32 devices in a mesh: groups: 2 (over y), span: 4 (over z), mp: 2 (over x), seq: 2 (over core).
Axes of the slice: x: 2, y: 2, z: 4, core: 2. Of those that a mesh axis runs over, the one named last changes fastest.
Arguments:
- query: bfloat16 [4, 8, 144, 3072], P(None, ('groups', 'span'), None, ('mp', 'seq')), parts along dimension 1, may hold values from -600 to 600
- noisy_kv: bfloat16 [4, 2, 8, 144, 3072], P(None, None, ('groups', 'span'), None, ('mp', 'seq')), parts along dimension 2, may hold values from -11 to 11
- clean_kv: bfloat16 [2, 8, 144, 3072], P(None, ('groups', 'span'), None, ('mp', 'seq')), parts along dimension 1, may hold values from -11 to 11
- causal_mask: int32 [8, 4], P('groups'), parts along dimension 0, may hold values from 0 to 1, as said below
- step_index: int32 [8, 4], P('groups'), parts along dimension 0, may hold values from 0 to 63, as said below
- finished: bfloat16 [8, 144, 3072], P(('groups', 'span'), None, ('mp', 'seq')), parts along dimension 0, may hold values from -6 to 6
- w_in: bfloat16 [3072, 512], P(('mp', 'seq')), may hold values from -0.109375 to 0.109375
- conv_w: bfloat16 [3, 512, 512], replicated, may hold values from -0.15625 to 0.15625
- fade_count: int32 [8], P(('groups', 'span')), parts along dimension 0, may hold values from 0 to 2, as said below
Outputs:
- attended: bfloat16 [4, 8, 144, 3072], P(None, ('groups', 'span'), None, ('mp', 'seq')), parts along dimension 1
- decoded: bfloat16 [8, 144, 512], P(('groups', 'span'), ('mp', 'seq')), parts along dimension 0
The draws below stay inside these ranges and needn't reach their ends.
There are 2 independent parts, one for each index of `groups`. The reference program is written for one: setup_inputs(seed, part) draws one part's arguments, and reference() takes and returns one part's arrays. A program takes and returns all parts, laid end to end along the dimension named above; an argument that names none is the same for every part. Nothing has to cross between parts.
Inputs may be any that keep to these rules, and one draw needn't show every extreme that they name: `causal_mask`: zero on and above the diagonal. `step_index`: each row counts up by one from its first entry; some row starts at 0 and some at 60. `fade_count`: some segment other than the first has 2.
All inputs are finite; a program needn't handle non-finite values.
Results may differ from the reference program's by a relative error of at most 0.015.
Values may be sent and summed in bfloat16 or wider, within the bound.
A program may use at most 64 MiB of HBM per device.

```python
import math
import jax
import jax.numpy as jnp
from jax import lax

FR = 6
SP = 24
CT = 144
HEADS = 24
HD = 128
DC = 512
KT = 3
FADE = 2
NSTEPS = 64
STEPS = 4
NSEG = 4


def head_gains():
    exponent = jnp.arange(HEADS).astype(jnp.float32) / (HEADS - 1) - 0.5
    gains = 3.0 ** exponent
    return jnp.repeat(gains, HD)


def attention_inputs(key):
    folded = jax.random.fold_in(key, 7)
    key_query, key_keys, key_values = jax.random.split(folded, 3)
    columns = HEADS * HD
    shape = (STEPS, NSEG, CT, columns)
    queries = jnp.clip(jax.random.normal(key_query, shape, jnp.float32), -6.0, 6.0)
    all_keys = jnp.clip(jax.random.normal(key_keys, shape, jnp.float32), -6.0, 6.0)
    values = jnp.clip(jax.random.normal(key_values, shape, jnp.float32), -6.0, 6.0)
    values = values * head_gains()
    return (queries, jnp.stack([all_keys, values], 1))


def draw_query(key, part):
    return attention_inputs(key)[0].astype(jnp.bfloat16)


def draw_noisy_kv(key, part):
    return attention_inputs(key)[1].astype(jnp.bfloat16)


def draw_clean_kv(key, part):
    folded = jax.random.fold_in(key, 13)
    key_keys, key_values = jax.random.split(folded, 2)
    shape = (NSEG, CT, HEADS * HD)
    all_keys = jnp.clip(jax.random.normal(key_keys, shape, jnp.float32), -6.0, 6.0)
    values = jnp.clip(jax.random.normal(key_values, shape, jnp.float32), -6.0, 6.0)
    values = values * head_gains()
    return jnp.stack([all_keys, values], 0).astype(jnp.bfloat16)


def draw_causal_mask(key, part):
    folded = jax.random.fold_in(key, 21)
    key_bits, key_row, key_col = jax.random.split(folded, 3)
    chosen = jax.random.randint(key_bits, (NSEG, NSEG), 0, 2)
    row_ids = jnp.arange(NSEG)[:, None]
    col_ids = jnp.arange(NSEG)[None, :]
    result = jnp.where((chosen > 0) & (row_ids > col_ids), 1, 0).astype(jnp.int32)
    forced_row = jax.random.randint(key_row, (), 1, NSEG)
    forced_col = jax.random.randint(key_col, (), 0, NSEG - 1)
    result = result.at[forced_row, 0].set(1)
    result = result.at[NSEG - 1, forced_col].set(1)
    return result.astype(jnp.int32)


def draw_step_index(key, part):
    folded = jax.random.fold_in(key, 31)
    key_first, key_spot = jax.random.split(folded, 2)
    first_index = jax.random.randint(key_first, (NSEG,), 0, NSTEPS - STEPS + 1)
    low_spot = jax.random.randint(key_spot, (), 0, NSEG)
    first_index = first_index.at[low_spot].set(0)
    first_index = first_index.at[(low_spot + 1) % NSEG].set(NSTEPS - STEPS)
    offsets = jnp.arange(STEPS).astype(jnp.int32)
    return (first_index[:, None] + offsets[None, :]).astype(jnp.int32)


def draw_fade_count(key, part):
    folded = jax.random.fold_in(key, 41)
    key_counts, key_spot = jax.random.split(folded, 2)
    counts = jax.random.randint(key_counts, (NSEG,), 0, FADE + 1)
    full_spot = jax.random.randint(key_spot, (), 1, NSEG)
    return counts.at[full_spot].set(FADE).astype(jnp.int32)


def block_scale(own_key, shape, cuts, low, high):
    def one(dim, blocks):
        steps = jax.random.uniform(jax.random.fold_in(jax.random.fold_in(own_key, 6), dim), (blocks,), jnp.float32, low / len(cuts), high / len(cuts))
        return jnp.repeat(jnp.exp(steps), shape[dim] // blocks).reshape((-1,) + (1,) * (len(shape) - dim - 1))

    gain = one(*cuts[0])
    for cut in cuts[1:]:
        gain = gain * one(*cut)
    return gain


def noise(own_key, dims, spread, limit, pieces=(), held_as=jnp.bfloat16):
    drawn = spread * jax.random.normal(own_key, dims, jnp.float32)
    if pieces:
        drawn = drawn * block_scale(own_key, dims, pieces, -0.22, 0.18)
    return jnp.clip(drawn, -limit, limit).astype(held_as)


def setup_inputs(seed: int = 0, part: int = 0) -> dict:
    key_list = jax.random.split(jax.random.key(seed), 10)
    part_splits = jax.random.split(jax.random.fold_in(key_list[9], part), 10)
    query = draw_query(jax.random.fold_in(jax.random.fold_in(key_list[9], part), 71), part)
    noisy_kv = draw_noisy_kv(jax.random.fold_in(jax.random.fold_in(key_list[9], part), 71), part)
    clean_kv = draw_clean_kv(jax.random.fold_in(jax.random.fold_in(key_list[9], part), 71), part)
    causal_mask = draw_causal_mask(jax.random.fold_in(jax.random.fold_in(key_list[9], part), 71), part)
    step_index = draw_step_index(jax.random.fold_in(jax.random.fold_in(key_list[9], part), 71), part)
    finished = noise(part_splits[5], (NSEG, CT, HEADS * HD), 1.0, 6.0, ((0, 4), (2, 4)))
    w_in = noise(key_list[6], (HEADS * HD, DC), (HEADS * HD) ** -0.5, 0.109375, ((0, 4),))
    conv_w = noise(key_list[7], (KT, DC, DC), (KT * DC) ** -0.5, 0.15625)
    fade_count = draw_fade_count(jax.random.fold_in(jax.random.fold_in(key_list[9], part), 71), part)
    return {"query": query, "noisy_kv": noisy_kv, "clean_kv": clean_kv, "causal_mask": causal_mask, "step_index": step_index, "finished": finished, "w_in": w_in, "conv_w": conv_w, "fade_count": fade_count}


def noise_level(indices):
    fraction = 1.0 - indices.astype(jnp.float32) / NSTEPS
    return 3.0 * fraction / (1.0 + 2.0 * fraction)

def rounded_copy(values):
    return lax.optimization_barrier(values.astype(jnp.bfloat16)).astype(jnp.float32)

def reference(query, noisy_kv, clean_kv, causal_mask, step_index, finished, w_in, conv_w, fade_count):
    scales = (0.5 + noise_level(step_index)) / math.sqrt(HD)
    clean_keys = clean_kv[0].reshape(NSEG * CT, HEADS, HD).astype(jnp.float32)
    clean_values = clean_kv[1].reshape(NSEG * CT, HEADS, HD).astype(jnp.float32)

    def one_segment(segment_id):
        queries = query[:, segment_id].reshape(STEPS, CT, HEADS, HD).astype(jnp.float32)
        own_keys = noisy_kv[:, 0, segment_id].reshape(STEPS, CT, HEADS, HD).astype(jnp.float32)
        own_values = noisy_kv[:, 1, segment_id].reshape(STEPS, CT, HEADS, HD).astype(jnp.float32)
        segment_scale = scales[segment_id][:, None, None, None]
        visible = jnp.repeat(causal_mask[segment_id], CT) > 0
        bias = jnp.where(visible, 0.0, -1e+30).astype(jnp.float32)
        own_scores = jnp.einsum('srhd,skhd->shrk', queries, own_keys) * segment_scale
        far_scores = jnp.einsum('srhd,khd->shrk', queries, clean_keys) * segment_scale + bias
        highest = jnp.maximum(own_scores.max(-1), far_scores.max(-1))[..., None]
        own_weights = jnp.exp(own_scores - highest)
        far_weights = jnp.exp(far_scores - highest)
        totals = own_weights.sum(-1) + far_weights.sum(-1)
        numer = jnp.einsum('shrk,skhd->shrd', rounded_copy(own_weights), own_values)
        numer = numer + jnp.einsum('shrk,khd->shrd', rounded_copy(far_weights), clean_values)
        averaged = numer / totals[..., None]
        normed = averaged * lax.rsqrt(lax.optimization_barrier(jnp.mean(averaged * averaged, axis=(1, 3), keepdims=True)) + 1e-06)
        return normed.transpose(0, 2, 1, 3).reshape(STEPS, CT, HEADS * HD).astype(jnp.bfloat16)
    per_segment = lax.map(one_segment, jnp.arange(NSEG))
    attended = jnp.transpose(per_segment, (1, 0, 2, 3))
    hidden = jnp.dot(finished.reshape(NSEG * CT, HEADS * HD), w_in, preferred_element_type=jnp.float32)
    hidden = hidden.astype(jnp.bfloat16).reshape(NSEG, SP, FR, DC)
    cache = jnp.concatenate([jnp.zeros((1, SP, KT - 1, DC), jnp.bfloat16), hidden[:-1, :, FR - KT + 1:]], 0)
    extended = jnp.concatenate([cache, hidden], 2)
    conv_total = jnp.zeros((NSEG * SP * FR, DC), jnp.float32)
    for tap_index in range(KT):
        window = extended[:, :, KT - 1 - tap_index:KT - 1 - tap_index + FR].reshape(NSEG * SP * FR, DC)
        conv_total = conv_total + jnp.dot(window, conv_w[tap_index], preferred_element_type=jnp.float32)
    frames = jax.nn.silu(conv_total).astype(jnp.bfloat16).reshape(NSEG, SP, FR, DC)
    tails = frames[:, :, FR - FADE:]
    prev_tails = jnp.concatenate([jnp.zeros((1, SP, FADE, DC), jnp.bfloat16), tails[:-1]], 0)
    padded = jnp.concatenate([prev_tails, jnp.zeros((NSEG, SP, FADE, DC), jnp.bfloat16)], 2)

    def align(pad_one, fade_one):
        return lax.dynamic_slice_in_dim(pad_one, (FADE - fade_one).astype(jnp.int32), FADE, 1)
    aligned = jax.vmap(align)(padded, fade_count)
    frame_pos = jnp.arange(FADE).astype(jnp.float32)
    fade_float = fade_count.astype(jnp.float32)[:, None]
    active = (frame_pos[None, :] < fade_float) & (jnp.arange(NSEG)[:, None] > 0)
    weights = jnp.where(active, (frame_pos[None, :] + 1.0) / (fade_float + 1.0), 1.0)
    head_frames = weights[:, None, :, None] * frames[:, :, :FADE].astype(jnp.float32)
    head_frames = head_frames + (1.0 - weights)[:, None, :, None] * aligned.astype(jnp.float32)
    blended = jnp.concatenate([head_frames, frames[:, :, FADE:].astype(jnp.float32)], 2)
    decoded = blended.astype(jnp.bfloat16).reshape(NSEG, CT, DC)
    return (attended, decoded)
```

```python
import functools
import math

import jax
import jax.numpy as jnp
from jax import lax
from jax.experimental import pallas as pl
from jax.experimental.pallas import tpu as pltpu
from jax.sharding import PartitionSpec as P

FR = 6
HEADS = 24
HD = 128
KT = 3
FADE = 2
NSTEPS = 64
MESH = pl.DeviceIdType.MESH
LOG2E = 1.4426950408889634
F32 = jnp.float32
BF16 = jnp.bfloat16


def nt_dot(a, b):
    return lax.dot_general(a, b, (((1,), (1,)), ((), ())), preferred_element_type=F32)


def tn_dot(a, b):
    return lax.dot_general(a, b, (((0,), (0,)), ((), ())), preferred_element_type=F32)


def kernel(
    dims,
    mask_hbm, index_hbm, fade_hbm, query_hbm, noisy_hbm, clean_hbm, fin_hbm, win_hbm, conv_hbm,
    att_ref, dec_ref,
    q_ref, noisy_ref, fin_ref, win_ref, conv_ref, own_ref, kv_ref,
    m_ref, l_ref, o_ref, part_ref, part_in, hid_ref, prev_ref, stat_ref, stat_in,
    mask_ref, index_ref, fade_ref,
    load_sem, own_sem, kv_send, kv_recv, part_send, part_recv, hid_send, hid_recv, stat_send, stat_recv,
):
    n, mp_n, seq_n, steps, ct, heads, rows, rp = dims
    group = mp_n * seq_n
    p = lax.axis_index("span")
    g = lax.axis_index("mp") * seq_n + lax.axis_index("seq")
    total = steps * ct

    def peer(d):
        other = lax.rem(g + d, group)
        return other, {"mp": other // seq_n, "seq": lax.rem(other, seq_n)}

    own_loads = []
    for h in range(heads):
        copy = pltpu.make_async_copy(
            clean_hbm.at[:, 0, :, pl.ds(h * HD, HD)], own_ref.at[h], own_sem.at[h]
        )
        copy.start()
        own_loads.append(copy)
    barrier = pltpu.get_barrier_semaphore()

    @pl.when(p > 0)
    def _():
        pl.semaphore_signal(barrier, inc=1, device_id={"span": p - 1}, device_id_type=MESH)

    @pl.when(p < n - 1)
    def _():
        pl.semaphore_signal(barrier, inc=1, device_id={"span": p + 1}, device_id_type=MESH)

    for d in range(1, group):
        pl.semaphore_signal(barrier, inc=1, device_id=peer(d)[1], device_id_type=MESH)

    ends = (p > 0).astype(jnp.int32) + (p < n - 1).astype(jnp.int32)
    pl.semaphore_wait(barrier, group - 1 + ends)

    def kv_copy(src, slot, h):
        return pltpu.make_async_remote_copy(
            src_ref=src, dst_ref=kv_ref.at[slot, h], send_sem=kv_send.at[slot, h],
            recv_sem=kv_recv.at[slot, h], device_id={"span": p + 1}, device_id_type=MESH,
        )

    for h in range(heads):
        own_loads[h].wait()

        @pl.when(p < n - 1)
        def _():
            kv_copy(own_ref.at[h], 0, h).start()

    loads = []
    for i, (src, dst) in enumerate(
        (
            (fin_hbm, fin_ref), (win_hbm, win_ref), (query_hbm, q_ref), (noisy_hbm, noisy_ref),
            (conv_hbm, conv_ref), (mask_hbm, mask_ref), (index_hbm, index_ref), (fade_hbm, fade_ref),
        )
    ):
        copy = pltpu.make_async_copy(src, dst, load_sem.at[i])
        copy.start()
        loads.append(copy)

    loads[0].wait()
    loads[1].wait()
    partial = jnp.dot(fin_ref[0], win_ref[...], preferred_element_type=F32).astype(BF16)
    row = lax.broadcasted_iota(jnp.int32, (rp, ct), 0)
    col = lax.broadcasted_iota(jnp.int32, (rp, ct), 1)
    for o in range(group):
        pick = jnp.where((row < rows) & (col == row + o * rows), 1.0, 0.0).astype(BF16)
        part_ref[o] = jnp.dot(pick, partial, preferred_element_type=F32).astype(BF16)

    for i in (2, 3, 5, 6, 7):
        loads[i].wait()
    lane = lax.broadcasted_iota(jnp.int32, (1, total), 1)
    indices = jnp.zeros((1, total), F32)
    for s in range(steps):
        value = index_ref[p, s].astype(F32)
        indices = jnp.where((lane >= s * ct) & (lane < (s + 1) * ct), value, indices)
    fraction = 1.0 - indices / NSTEPS
    level = 3.0 * fraction / (1.0 + 2.0 * fraction)
    scale = (0.5 + level) * (LOG2E / math.sqrt(HD))

    def own_head(h):
        cols = slice(h * HD, (h + 1) * HD)
        ms, ls, os = [], [], []
        for s in range(steps):
            step_index = jnp.full((1, ct), index_ref[p, s].astype(F32), F32)
            part = 1.0 - step_index / NSTEPS
            own_scale = (0.5 + 3.0 * part / (1.0 + 2.0 * part)) * (LOG2E / math.sqrt(HD))
            scores = nt_dot(noisy_ref[s, 0, 0, :, cols], q_ref[s, 0, :, cols]) * own_scale
            m = scores.max(0, keepdims=True)
            w = jnp.exp2(scores - m)
            ms.append(m)
            ls.append(w.sum(0, keepdims=True))
            os.append(tn_dot(noisy_ref[s, 1, 0, :, cols], w.astype(BF16)))
        m_ref[h] = jnp.concatenate(ms, 1)
        l_ref[h] = jnp.concatenate(ls, 1)
        o_ref[h] = jnp.concatenate(os, 1)

    def part_copy(d):
        other, where = peer(d)
        return pltpu.make_async_remote_copy(
            src_ref=part_ref.at[other], dst_ref=part_in.at[d - 1], send_sem=part_send.at[d - 1],
            recv_sem=part_recv.at[d - 1], device_id=where, device_id_type=MESH,
        )

    hid_copy = pltpu.make_async_remote_copy(
        src_ref=hid_ref, dst_ref=prev_ref, send_sem=hid_send, recv_sem=hid_recv,
        device_id={"span": p + 1}, device_id_type=MESH,
    )

    for h in range(heads):
        own_head(h)
        if h == 0:
            for d in range(1, group):
                part_copy(d).start()
        if h == heads // 2:
            for d in range(1, group):
                part_copy(d).wait()
            summed = part_ref[g].astype(F32)
            for d in range(1, group):
                summed = summed + part_in[d - 1].astype(F32)
            hid_ref[...] = summed.astype(BF16)
    loads[4].wait()

    @pl.when(p < n - 1)
    def _():
        hid_copy.start()

    def absorb(j, h):
        cols = slice(h * HD, (h + 1) * HD)
        queries = q_ref[:, 0, :, cols].reshape(total, HD)
        visible = mask_ref[p, p - 1 - j]
        bias = jnp.where(visible > 0, 0.0, -1e30).astype(F32)
        scores = nt_dot(kv_ref[j, h, 0], queries) * scale + bias
        old = m_ref[h]
        m = jnp.maximum(old, scores.max(0, keepdims=True))
        factor = jnp.exp2(old - m)
        w = jnp.exp2(scores - m)
        m_ref[h] = m
        l_ref[h] = l_ref[h] * factor + w.sum(0, keepdims=True)
        o_ref[h] = o_ref[h] * factor + tn_dot(kv_ref[j, h, 1], w.astype(BF16))

    def block(j, carry):
        for h in range(heads):
            kv_copy(own_ref.at[h], j, h).wait_recv()

            @pl.when(p < n - 1)
            def _():
                kv_copy(kv_ref.at[j, h], j + 1, h).start()

            absorb(j, h)
        return carry

    def decode():
        @pl.when(p > 0)
        def _():
            hid_copy.wait_recv()

        @pl.when(p == 0)
        def _():
            prev_ref[...] = jnp.zeros_like(prev_ref)

        now = hid_ref[...].astype(F32)
        before = prev_ref[...].astype(F32)
        width = now.shape[1]
        frame = lax.rem(lax.broadcasted_iota(jnp.int32, (rp, width), 0), FR)
        mixed = jnp.zeros((2 * rp, width), F32)
        for k in range(KT):
            late = pltpu.roll(before, k, 0) if k else before
            if k:
                cur = jnp.where(
                    frame >= k, pltpu.roll(now, k, 0), pltpu.roll(before, rp + k - FR, 0)
                )
            else:
                cur = now
            window = jnp.concatenate([cur, late], 0).astype(BF16)
            mixed = mixed + jnp.dot(window, conv_ref[k], preferred_element_type=F32)
        frames = jax.nn.silu(mixed).astype(BF16).astype(F32)
        cur, late = frames[:rp], frames[rp:]
        fade = fade_ref[0]
        aligned = jnp.zeros_like(late)
        for count in range(1, FADE + 1):
            aligned = jnp.where(fade == count, pltpu.roll(late, rp - FR + count, 0), aligned)
        active = (frame < fade) & (p > 0)
        fade_f = fade.astype(F32)
        weight = (frame.astype(F32) + 1.0) / (jnp.zeros((rp, width), F32) + fade_f + 1.0)
        mix = weight * cur + (1.0 - weight) * aligned
        dec_ref[0] = jnp.where(active, mix, cur)[:rows].astype(BF16)

    first = jnp.minimum(p, 1)
    lax.fori_loop(0, first, block, 0)
    decode()
    lax.fori_loop(first, p, block, 0)

    squares = jnp.zeros((1, total), F32)
    for h in range(heads):
        averaged = o_ref[h] / l_ref[h]
        o_ref[h] = averaged
        squares = squares + jnp.sum(averaged * averaged, 0, keepdims=True)
    stat_ref[...] = squares

    def stat_copy(d):
        return pltpu.make_async_remote_copy(
            src_ref=stat_ref, dst_ref=stat_in.at[d - 1], send_sem=stat_send.at[d - 1],
            recv_sem=stat_recv.at[d - 1], device_id=peer(d)[1], device_id_type=MESH,
        )

    for d in range(1, group):
        stat_copy(d).start()
    for d in range(1, group):
        stat_copy(d).wait()
    for d in range(1, group):
        squares = squares + stat_in[d - 1]
    inverse = lax.rsqrt(squares / (HD * heads * group) + 1e-06)
    for h in range(heads):
        normed = jnp.transpose(o_ref[h] * inverse).astype(BF16)
        for s in range(steps):
            att_ref[s, 0, :, h * HD : (h + 1) * HD] = normed[s * ct : (s + 1) * ct]

    @pl.when(p < n - 1)
    def _():
        hid_copy.wait_send()

        def drain(j, carry):
            for h in range(heads):
                kv_copy(own_ref.at[h], j, h).wait_send()
            return carry

        lax.fori_loop(0, p + 1, drain, 0)


def write_out(att_ref, dec_ref, att_hbm, dec_hbm, sem):
    copies = [
        pltpu.make_async_copy(att_ref, att_hbm, sem.at[0]),
        pltpu.make_async_copy(dec_ref, dec_hbm, sem.at[1]),
    ]
    for copy in copies:
        copy.start()
    for copy in copies:
        copy.wait()


def per_device(sizes, query, noisy_kv, clean_kv, causal_mask, step_index, finished, w_in, conv_w, fade_count):
    n, mp_n, seq_n = sizes
    group = mp_n * seq_n
    steps, _, ct, width = query.shape
    heads = width // HD
    channels = w_in.shape[1]
    rows = ct // group
    rp = -(-rows // 16) * 16
    total = steps * ct
    dims = (n, mp_n, seq_n, steps, ct, heads, rows, rp)
    vmem = pltpu.VMEM
    dma = pltpu.SemaphoreType.DMA
    hbm = pl.BlockSpec(memory_space=pltpu.HBM)
    out = pl.BlockSpec(memory_space=pltpu.VMEM)
    slots = max(n - 1, 1)
    arguments = [
        pltpu.with_memory_space_constraint(x, pltpu.HBM)
        for x in (causal_mask, step_index, query, noisy_kv, clean_kv, finished, w_in, conv_w)
    ]
    arguments.insert(2, fade_count)
    attended, decoded = pl.pallas_call(
        functools.partial(kernel, dims),
        out_shape=(
            jax.ShapeDtypeStruct(query.shape, BF16),
            jax.ShapeDtypeStruct((1, rows, channels), BF16),
        ),
        in_specs=[hbm] * 9,
        out_specs=(out, out),
        scratch_shapes=[
            vmem(query.shape, BF16),
            vmem(noisy_kv.shape, BF16),
            vmem(finished.shape, BF16),
            vmem(w_in.shape, BF16),
            vmem(conv_w.shape, BF16),
            vmem((heads, 2, ct, HD), BF16),
            vmem((slots, heads, 2, ct, HD), BF16),
            vmem((heads, 1, total), F32),
            vmem((heads, 1, total), F32),
            vmem((heads, HD, total), F32),
            vmem((group, rp, channels), BF16),
            vmem((group - 1, rp, channels), BF16),
            vmem((rp, channels), BF16),
            vmem((rp, channels), BF16),
            vmem((1, total), F32),
            vmem((group - 1, 1, total), F32),
            pltpu.SMEM(causal_mask.shape, jnp.int32),
            pltpu.SMEM(step_index.shape, jnp.int32),
            pltpu.SMEM(fade_count.shape, jnp.int32),
            dma((8,)),
            dma((heads,)),
            dma((slots, heads)),
            dma((slots, heads)),
            dma((group - 1,)),
            dma((group - 1,)),
            dma,
            dma,
            dma((group - 1,)),
            dma((group - 1,)),
        ],
        compiler_params=pltpu.CompilerParams(
            collective_id=0, has_side_effects=True, vmem_limit_bytes=28 * 2**20
        ),
    )(*arguments)
    return pl.pallas_call(
        write_out,
        out_shape=(
            jax.ShapeDtypeStruct(attended.shape, BF16),
            jax.ShapeDtypeStruct(decoded.shape, BF16),
        ),
        in_specs=[out, out],
        out_specs=(hbm, hbm),
        scratch_shapes=[dma((2,))],
        compiler_params=pltpu.CompilerParams(vmem_limit_bytes=4 * 2**20),
    )(attended, decoded)


def solution(mesh):
    placed = (
        P(None, ("groups", "span"), None, ("mp", "seq")),
        P(None, None, ("groups", "span"), None, ("mp", "seq")),
        P(None, ("groups", "span"), None, ("mp", "seq")),
        P("groups", None),
        P("groups", None),
        P(("groups", "span"), None, ("mp", "seq")),
        P(("mp", "seq"), None),
        P(),
        P(("groups", "span")),
    )
    sizes = (mesh.shape["span"], mesh.shape["mp"], mesh.shape["seq"])
    return jax.shard_map(
        functools.partial(per_device, sizes),
        mesh=mesh,
        in_specs=placed,
        out_specs=(
            P(None, ("groups", "span"), None, ("mp", "seq")),
            P(("groups", "span"), ("mp", "seq"), None),
        ),
        check_vma=False,
    )
```

```python
import functools
import math

import jax
import jax.numpy as jnp
from jax import lax
from jax.experimental import pallas as pl
from jax.experimental.pallas import tpu as pltpu
from jax.sharding import PartitionSpec as P

FR = 6
HD = 128
KT = 3
FADE = 2
NSTEPS = 64
LANES = 128
MESH = pl.DeviceIdType.MESH
LOG2E = 1.4426950408889634
LOW = -1e30
F32 = jnp.float32
BF16 = jnp.bfloat16


def nt_dot(a, b):
    return lax.dot_general(a, b, (((1,), (1,)), ((), ())), preferred_element_type=F32)


def tn_dot(a, b):
    return lax.dot_general(a, b, (((0,), (0,)), ((), ())), preferred_element_type=F32)


def head_cols(h):
    return pl.ds(pl.multiple_of(h * HD, HD), HD)


def kernel(
    dims,
    mask_hbm, index_hbm, fade_hbm, query_hbm, noisy_hbm, clean_hbm, fin_hbm, win_hbm, conv_hbm,
    avg_ref, inv_ref, dec_ref,
    q_ref, noisy_ref, fin_ref, win_ref, conv_ref, own_ref, kv_ref, lastq_ref,
    m_ref, l_ref, o_ref, osend_ref, oin_ref, mlsend_ref, mlin_ref,
    part_ref, part_in, hid_ref, prev_ref, sq_ref, stat_in, mask_ref, index_ref, fade_ref,
    load_sem, kv_send, kv_recv, lastq_send, lastq_recv, o_send, o_recv, ml_send, ml_recv,
    part_send, part_recv, hid_send, hid_recv, stat_send, stat_recv,
):
    n, mp_n, seq_n, steps, ct, heads, rows, rp, main = dims
    group = mp_n * seq_n
    rest = ct - main
    total = steps * ct
    p = lax.axis_index("span")
    g = lax.axis_index("mp") * seq_n + lax.axis_index("seq")
    last, helper = n - 1, n - 2
    feeds = p < helper
    helps = p == helper
    ends = (p == last) & (n > 1)
    blocks = max(helper, 0)
    routed = min(2, heads) if n > 1 else 0

    def peer(d):
        other = lax.rem(g + d, group)
        return other, {"mp": other // seq_n, "seq": lax.rem(other, seq_n)}

    barrier = pltpu.get_barrier_semaphore()

    @pl.when(p > 0)
    def _():
        pl.semaphore_signal(barrier, inc=1, device_id={"span": p - 1}, device_id_type=MESH)

    @pl.when(p < n - 1)
    def _():
        pl.semaphore_signal(barrier, inc=1, device_id={"span": p + 1}, device_id_type=MESH)

    for d in range(1, group):
        pl.semaphore_signal(barrier, inc=1, device_id=peer(d)[1], device_id_type=MESH)

    near = (p > 0).astype(jnp.int32) + (p < n - 1).astype(jnp.int32)
    loads = []
    for i, (src, dst) in enumerate(
        (
            (fin_hbm, fin_ref), (win_hbm, win_ref), (query_hbm, q_ref), (noisy_hbm, noisy_ref),
            (mask_hbm, mask_ref), (index_hbm, index_ref), (fade_hbm, fade_ref), (conv_hbm, conv_ref),
            (clean_hbm, own_ref),
        )
    ):
        loads.append(pltpu.make_async_copy(src, dst, load_sem.at[i]))
    for copy in loads[:2]:
        copy.start()

    pl.semaphore_wait(barrier, group - 1 + near)

    def kv_copy(src, slot, h):
        return pltpu.make_async_remote_copy(
            src_ref=src, dst_ref=kv_ref.at[slot, h], send_sem=kv_send.at[slot, h],
            recv_sem=kv_recv.at[slot, h], device_id={"span": p + 1}, device_id_type=MESH,
        )

    def own_kv_copy(h):
        return kv_copy(clean_hbm.at[:, 0, :, head_cols(h)], 0, h)

    def lastq_copy(h):
        return pltpu.make_async_remote_copy(
            src_ref=query_hbm.at[:, 0, :, head_cols(h)], dst_ref=lastq_ref.at[h],
            send_sem=lastq_send.at[h], recv_sem=lastq_recv.at[h],
            device_id={"span": p - 1}, device_id_type=MESH,
        )

    def o_copy(h):
        return pltpu.make_async_remote_copy(
            src_ref=osend_ref.at[h], dst_ref=oin_ref.at[h], send_sem=o_send.at[h],
            recv_sem=o_recv.at[h], device_id={"span": p + 1}, device_id_type=MESH,
        )

    def ml_copy(h):
        return pltpu.make_async_remote_copy(
            src_ref=mlsend_ref.at[h], dst_ref=mlin_ref.at[h], send_sem=ml_send.at[h],
            recv_sem=ml_recv.at[h], device_id={"span": p + 1}, device_id_type=MESH,
        )

    def part_copy(d):
        other, where = peer(d)
        return pltpu.make_async_remote_copy(
            src_ref=part_ref.at[other], dst_ref=part_in.at[d - 1], send_sem=part_send.at[d - 1],
            recv_sem=part_recv.at[d - 1], device_id=where, device_id_type=MESH,
        )

    def stat_copy(d):
        return pltpu.make_async_remote_copy(
            src_ref=sq_ref, dst_ref=stat_in.at[d - 1], send_sem=stat_send.at[d - 1],
            recv_sem=stat_recv.at[d - 1], device_id=peer(d)[1], device_id_type=MESH,
        )

    hid_copy = pltpu.make_async_remote_copy(
        src_ref=hid_ref, dst_ref=prev_ref, send_sem=hid_send, recv_sem=hid_recv,
        device_id={"span": p + 1}, device_id_type=MESH,
    )

    def every_head(body, first=0):
        lax.fori_loop(first, heads, lambda h, c: (body(h), c)[1], 0)

    ahead = max(routed, 1)

    @pl.when(feeds)
    def _():
        for h in range(ahead):
            own_kv_copy(h).start()

    @pl.when(helps)
    def _():
        for h in range(routed):
            own_kv_copy(h).start()

    @pl.when(ends)
    def _():
        every_head(lambda h: lastq_copy(h).start(), routed)

    for copy in loads[2:8]:
        copy.start()

    @pl.when(helps)
    def _():
        loads[8].start()

    def arrive(j, h):
        kv_copy(kv_ref.at[j, h], j, h).wait_recv()

    def hand_on(j, h):
        arrive(j, h)
        kv_copy(kv_ref.at[j, h], j + 1, h).start()

    def pass_on(h):
        lax.fori_loop(0, p, lambda j, c: (hand_on(j, h), c)[1], 0)

        @pl.when((h + 1 >= ahead) & (h + 1 < heads))
        def _():
            own_kv_copy(h + 1).start()

    @pl.when(feeds)
    def _():
        for h in range(ahead):
            pass_on(h)

    loads[0].wait()
    loads[1].wait()
    partial = jnp.dot(fin_ref[0], win_ref[...], preferred_element_type=F32).astype(BF16)
    row = lax.broadcasted_iota(jnp.int32, (rp, ct), 0)
    col = lax.broadcasted_iota(jnp.int32, (rp, ct), 1)
    for o in range(group):
        pick = jnp.where((row < rows) & (col == row + o * rows), 1.0, 0.0).astype(BF16)
        part_ref[o] = jnp.dot(pick, partial, preferred_element_type=F32).astype(BF16)
    for d in range(1, group):
        part_copy(d).start()

    for i in (2, 3, 4, 5, 6):
        loads[i].wait()

    @pl.when(helps)
    def _():
        loads[8].wait()

    lane = lax.broadcasted_iota(jnp.int32, (1, total), 1)
    split = steps * main
    step_of = jnp.zeros((1, total), jnp.int32)
    for s in range(1, steps):
        step_of = step_of + (
            ((lane >= s * main) & (lane < split)) | (lane >= split + s * rest)
        ).astype(jnp.int32)

    def scale_row(segment):
        indices = jnp.zeros((1, total), F32)
        for s in range(steps):
            indices = jnp.where(step_of == s, index_ref[segment, s].astype(F32), indices)
        fraction = 1.0 - indices / NSTEPS
        level = 3.0 * fraction / (1.0 + 2.0 * fraction)
        return (0.5 + level) * (LOG2E / math.sqrt(HD))

    scale = scale_row(p)
    last_scale = scale_row(last)

    wide = 4
    tiles = []
    for s in range(0, steps if main else 0, wide):
        held = range(s, min(s + wide, steps))
        tiles.append((s * main, len(held) * main, [(k, 0, main) for k in held]))
    if rest:
        tiles.append((split, steps * rest, [(s, main, ct) for s in range(steps)]))

    def query_tile(t, row):
        return jnp.concatenate([row(*piece) for piece in tiles[t][2]], 0)

    def own_query(h):
        return lambda s, lo, hi: q_ref[s, 0, lo:hi, head_cols(h)]

    def last_query(h):
        return lambda s, lo, hi: lastq_ref[h, s, lo:hi, :]

    def part_of(ref, tile):
        return ref[:, tile[0] : tile[0] + tile[1]]

    def one_pass(c, scored, old=None):
        tops = []
        for scores, _, visible in scored:
            top = scores.max(0, keepdims=True) * c
            tops.append(top if visible is None else jnp.where(visible > 0, top, LOW))
        m = functools.reduce(jnp.maximum, tops)
        if old is not None:
            m = jnp.maximum(m, old[0])
        l, o = 0.0, 0.0
        for scores, values, visible in scored:
            base = m if visible is None else jnp.where(visible > 0, m, -LOW)
            w = jnp.exp2(scores * c - base)
            l = l + w.sum(0, keepdims=True)
            o = o + values(w)
        if old is not None:
            factor = jnp.exp2(old[0] - m)
            l = l + old[1] * factor
            o = o + old[2] * factor
        return m, l, o

    def plain(keys, values, queries, visible):
        return nt_dot(keys, queries), lambda w: tn_dot(values, w.astype(BF16)), visible

    def noisy(h, t, queries):
        keys = lambda s: noisy_ref[s, 0, 0, :, head_cols(h)]
        values = lambda s: noisy_ref[s, 1, 0, :, head_cols(h)]
        if tiles[t][0] < split:
            pieces = [k for k, _, _ in tiles[t][2]]
            cut = lambda x, i: x[:, i * main : (i + 1) * main]
            scores = jnp.concatenate(
                [nt_dot(keys(k), queries[i * main : (i + 1) * main]) for i, k in enumerate(pieces)], 1
            )
            return scores, lambda w: jnp.concatenate(
                [tn_dot(values(k), cut(w, i).astype(BF16)) for i, k in enumerate(pieces)], 1
            ), None
        owner = lax.broadcasted_iota(jnp.int32, (ct, steps * rest), 1) // rest
        scores = nt_dot(keys(0), queries)
        for s in range(1, steps):
            scores = jnp.where(owner == s, nt_dot(keys(s), queries), scores)

        def weigh(w):
            o = 0.0
            for s in range(steps):
                o = o + tn_dot(values(s), jnp.where(owner == s, w, 0.0).astype(BF16))
            return o

        return scores, weigh, None

    def own_state(h):
        for t, tile in enumerate(tiles):
            queries = query_tile(t, own_query(h))
            m, l, o = one_pass(part_of(scale, tile), [noisy(h, t, queries)])
            cols = slice(tile[0], tile[0] + tile[1])
            m_ref[h, :, cols], l_ref[h, :, cols], o_ref[h, :, cols] = m, l, o

    def own_update(j, h):
        visible = mask_ref[p, p - 1 - j]
        for t, tile in enumerate(tiles):
            queries = query_tile(t, own_query(h))
            cols = slice(tile[0], tile[0] + tile[1])
            old = m_ref[h, :, cols], l_ref[h, :, cols], o_ref[h, :, cols]
            block = plain(kv_ref[j, h, 0], kv_ref[j, h, 1], queries, visible)
            m, l, o = one_pass(part_of(scale, tile), [block], old)
            m_ref[h, :, cols], l_ref[h, :, cols], o_ref[h, :, cols] = m, l, o

    def finish_tile(h, t, averaged):
        lo, width, pieces = tiles[t]
        sq_ref[:, lo : lo + width] += jnp.sum(averaged * averaged, 0, keepdims=True)
        turned = jnp.transpose(averaged)
        at = 0
        for s, first, end in pieces:
            avg_ref[s, 0, first:end, head_cols(h)] = turned[at : at + end - first]
            at += end - first

    def finish_own(h):
        for t, tile in enumerate(tiles):
            cols = slice(tile[0], tile[0] + tile[1])
            finish_tile(h, t, o_ref[h, :, cols] * (1.0 / l_ref[h, :, cols]))

    fold = LANES // (steps * rest) if rest else 1

    def pack(h, t, o):
        lo, width, _ = tiles[t]
        if lo < split:
            for i in range(width // LANES):
                at = (lo // LANES + i) * HD
                osend_ref[h, at : at + HD, :] = o[:, i * LANES : (i + 1) * LANES].astype(BF16)
        else:
            high, at = HD // fold, split // LANES * HD
            pieces = [o[i * high : (i + 1) * high] for i in range(fold)]
            osend_ref[h, at : at + high, :] = jnp.concatenate(pieces, 1).astype(BF16)

    def unpack(h, t):
        lo, width, _ = tiles[t]
        if lo < split:
            pieces = []
            for i in range(width // LANES):
                at = (lo // LANES + i) * HD
                pieces.append(oin_ref[h, at : at + HD, :].astype(F32))
            return jnp.concatenate(pieces, 1)
        high, at = HD // fold, split // LANES * HD
        held = oin_ref[h, at : at + high, :].astype(F32)
        return jnp.concatenate([held[:, i * width : (i + 1) * width] for i in range(fold)], 0)

    def finish_last(h):
        ml_copy(h).wait_recv()
        o_copy(h).wait_recv()
        for t, tile in enumerate(tiles):
            cols = slice(tile[0], tile[0] + tile[1])
            mine, theirs = m_ref[h, :, cols], mlin_ref[h, 0, :, cols]
            m = jnp.maximum(mine, theirs)
            a, b = jnp.exp2(mine - m), jnp.exp2(theirs - m)
            inverse = 1.0 / (l_ref[h, :, cols] * a + mlin_ref[h, 1, :, cols] * b)
            finish_tile(h, t, o_ref[h, :, cols] * (a * inverse) + unpack(h, t) * (b * inverse))

    together = min(blocks, 3)

    def help_sums(h, c, first, queries, segment):
        def arrived(j):
            visible = mask_ref[segment, helper - 1 - j]
            return plain(kv_ref[j, h, 0], kv_ref[j, h, 1], queries, visible)

        sums = one_pass(c, [first] + [arrived(j) for j in range(together)])
        if blocks > together:
            sums = lax.fori_loop(
                together, blocks, lambda j, old: one_pass(c, [arrived(j)], old), sums
            )
        return sums

    def help_last(h):
        for t, tile in enumerate(tiles):
            queries = query_tile(t, last_query(h))
            own = plain(
                own_ref[0, 0, :, head_cols(h)], own_ref[1, 0, :, head_cols(h)], queries,
                mask_ref[last, helper],
            )
            m, l, o = help_sums(h, part_of(last_scale, tile), own, queries, last)
            cols = slice(tile[0], tile[0] + tile[1])
            mlsend_ref[h, 0, :, cols], mlsend_ref[h, 1, :, cols] = m, l
            pack(h, t, o)

    def help_own(h):
        for t, tile in enumerate(tiles):
            queries = query_tile(t, own_query(h))
            m, l, o = help_sums(h, part_of(scale, tile), noisy(h, t, queries), queries, helper)
            finish_tile(h, t, o * (1.0 / l))

    def gather_hidden():
        for d in range(1, group):
            part_copy(d).wait()
        summed = part_ref[g].astype(F32)
        for d in range(1, group):
            summed = summed + part_in[d - 1].astype(F32)
        hid_ref[...] = summed.astype(BF16)

        @pl.when(p < n - 1)
        def _():
            hid_copy.start()

    def update_all(h):
        lax.fori_loop(0, p, lambda j, c: (own_update(j, h), c)[1], 0)

    def first_heads(h):
        @pl.when(feeds & (h + ahead < heads))
        def _():
            pass_on(h + ahead)

        @pl.when(jnp.logical_not(helps) & (h == min(1, heads - 1)))
        def _():
            gather_hidden()

        @pl.when(helps)
        def _():
            @pl.when(h >= routed)
            def _():
                lax.fori_loop(0, blocks, lambda j, c: (arrive(j, h), c)[1], 0)
                lastq_copy(h).wait_recv()
                help_last(h)
                ml_copy(h).start()
                o_copy(h).start()

            help_own(h)

        @pl.when(jnp.logical_not(helps))
        def _():
            own_state(h)

        @pl.when(jnp.logical_not(helps | ends))
        def _():
            update_all(h)
            finish_own(h)

    def last_routed(h):
        lax.fori_loop(0, p, lambda j, c: (arrive(j, h), c)[1], 0)
        update_all(h)
        finish_own(h)

    def decode():
        loads[7].wait()

        @pl.when(p > 0)
        def _():
            hid_copy.wait_recv()

        @pl.when(p == 0)
        def _():
            prev_ref[...] = jnp.zeros_like(prev_ref)

        now = hid_ref[...].astype(F32)
        before = prev_ref[...].astype(F32)
        width = now.shape[1]
        frame = lax.rem(lax.broadcasted_iota(jnp.int32, (rp, width), 0), FR)
        mixed = jnp.zeros((2 * rp, width), F32)
        for k in range(KT):
            late = pltpu.roll(before, k, 0) if k else before
            if k:
                cur = jnp.where(
                    frame >= k, pltpu.roll(now, k, 0), pltpu.roll(before, rp + k - FR, 0)
                )
            else:
                cur = now
            window = jnp.concatenate([cur, late], 0).astype(BF16)
            mixed = mixed + jnp.dot(window, conv_ref[k], preferred_element_type=F32)
        frames = jax.nn.silu(mixed).astype(BF16).astype(F32)
        cur, late = frames[:rp], frames[rp:]
        fade = fade_ref[0]
        aligned = jnp.zeros_like(late)
        for count in range(1, FADE + 1):
            aligned = jnp.where(fade == count, pltpu.roll(late, rp - FR + count, 0), aligned)
        active = (frame < fade) & (p > 0)
        fade_f = fade.astype(F32)
        weight = (frame.astype(F32) + 1.0) / (jnp.zeros((rp, width), F32) + fade_f + 1.0)
        mix = weight * cur + (1.0 - weight) * aligned
        dec_ref[0] = jnp.where(active, mix, cur)[:rows].astype(BF16)

    sq_ref[...] = jnp.zeros_like(sq_ref)

    @pl.when(helps)
    def _():
        def hand_on_routed(j, carry):
            for h in range(routed):
                hand_on(j, h)
            return carry

        lax.fori_loop(0, min(blocks, 1), hand_on_routed, 0)
        gather_hidden()
        lax.fori_loop(min(blocks, 1), blocks, hand_on_routed, 0)

    every_head(first_heads)
    decode()

    @pl.when(ends)
    def _():
        for h in range(routed):
            last_routed(h)
        every_head(finish_last, routed)

    for d in range(1, group):
        stat_copy(d).start()
    for d in range(1, group):
        stat_copy(d).wait()
    squares = sq_ref[...]
    for d in range(1, group):
        squares = squares + stat_in[d - 1]
    inv_ref[...] = lax.rsqrt(squares / (HD * heads * group) + 1e-06)

    @pl.when(p < n - 1)
    def _():
        hid_copy.wait_send()

    def drain_kv(h):
        def one(j, carry):
            kv_copy(clean_hbm.at[:, 0, :, head_cols(h)], j, h).wait_send()
            return carry

        lax.fori_loop(0, p + 1, one, 0)

    @pl.when(feeds)
    def _():
        every_head(drain_kv)

    @pl.when(helps)
    def _():
        for h in range(routed):
            drain_kv(h)

        def drain(h):
            ml_copy(h).wait_send()
            o_copy(h).wait_send()

        every_head(drain, routed)

    @pl.when(ends)
    def _():
        every_head(lambda h: lastq_copy(h).wait_send(), routed)


def write_out(dims, avg_ref, inv_ref, dec_ref, att_hbm, dec_hbm, att_ref, sem):
    steps, ct, heads, main = dims
    rest, split = ct - main, steps * main
    dec_copy = pltpu.make_async_copy(dec_ref, dec_hbm, sem.at[steps])
    dec_copy.start()
    inverse = jnp.transpose(jnp.broadcast_to(inv_ref[...], (HD, steps * ct)))
    copies = []
    for s in range(steps):
        spans = [(0, main, s * main)] if main else []
        if rest:
            spans.append((main, ct, split + s * rest))
        for lo, hi, at in spans:
            for h in range(heads):
                cols = slice(h * HD, (h + 1) * HD)
                att_ref[s, 0, lo:hi, cols] = (
                    avg_ref[s, 0, lo:hi, cols] * inverse[at : at + hi - lo]
                ).astype(BF16)
        copy = pltpu.make_async_copy(att_ref.at[s], att_hbm.at[s], sem.at[s])
        copy.start()
        copies.append(copy)
    for copy in copies:
        copy.wait()
    dec_copy.wait()


def per_device(sizes, query, noisy_kv, clean_kv, causal_mask, step_index, finished, w_in, conv_w, fade_count):
    n, mp_n, seq_n = sizes
    group = mp_n * seq_n
    steps, _, ct, width = query.shape
    heads = width // HD
    channels = w_in.shape[1]
    rows = ct // group
    rp = -(-rows // 16) * 16
    main = ct // LANES * LANES
    total = steps * ct
    dims = (n, mp_n, seq_n, steps, ct, heads, rows, rp, main)
    vmem = pltpu.VMEM
    dma = pltpu.SemaphoreType.DMA
    hbm = pl.BlockSpec(memory_space=pltpu.HBM)
    out = pl.BlockSpec(memory_space=pltpu.VMEM)
    slots = max(n - 1, 1)
    arguments = [
        pltpu.with_memory_space_constraint(x, pltpu.HBM)
        for x in (causal_mask, step_index, query, noisy_kv, clean_kv, finished, w_in, conv_w)
    ]
    arguments.insert(2, fade_count)
    averaged, inverse, decoded = pl.pallas_call(
        functools.partial(kernel, dims),
        out_shape=(
            jax.ShapeDtypeStruct(query.shape, F32),
            jax.ShapeDtypeStruct((1, total), F32),
            jax.ShapeDtypeStruct((1, rows, channels), BF16),
        ),
        in_specs=[hbm] * 9,
        out_specs=(out, out, out),
        scratch_shapes=[
            vmem(query.shape, BF16),
            vmem(noisy_kv.shape, BF16),
            vmem(finished.shape, BF16),
            vmem(w_in.shape, BF16),
            vmem(conv_w.shape, BF16),
            vmem(clean_kv.shape, BF16),
            vmem((slots, heads, 2, ct, HD), BF16),
            vmem((heads, steps, ct, HD), BF16),
            vmem((heads, 1, total), F32),
            vmem((heads, 1, total), F32),
            vmem((heads, HD, total), F32),
            vmem((heads, total * HD // LANES, LANES), BF16),
            vmem((heads, total * HD // LANES, LANES), BF16),
            vmem((heads, 2, 1, total), F32),
            vmem((heads, 2, 1, total), F32),
            vmem((group, rp, channels), BF16),
            vmem((group - 1, rp, channels), BF16),
            vmem((rp, channels), BF16),
            vmem((rp, channels), BF16),
            vmem((1, total), F32),
            vmem((group - 1, 1, total), F32),
            pltpu.SMEM(causal_mask.shape, jnp.int32),
            pltpu.SMEM(step_index.shape, jnp.int32),
            pltpu.SMEM(fade_count.shape, jnp.int32),
            dma((9,)),
            dma((slots, heads)),
            dma((slots, heads)),
            dma((heads,)),
            dma((heads,)),
            dma((heads,)),
            dma((heads,)),
            dma((heads,)),
            dma((heads,)),
            dma((group - 1,)),
            dma((group - 1,)),
            dma,
            dma,
            dma((group - 1,)),
            dma((group - 1,)),
        ],
        compiler_params=pltpu.CompilerParams(
            collective_id=0, has_side_effects=True, vmem_limit_bytes=28 * 2**20
        ),
    )(*arguments)
    return pl.pallas_call(
        functools.partial(write_out, (steps, ct, heads, main)),
        out_shape=(
            jax.ShapeDtypeStruct(query.shape, BF16),
            jax.ShapeDtypeStruct(decoded.shape, BF16),
        ),
        in_specs=[out] * 3,
        out_specs=(hbm, hbm),
        scratch_shapes=[vmem(query.shape, BF16), dma((steps + 1,))],
        compiler_params=pltpu.CompilerParams(vmem_limit_bytes=8 * 2**20),
    )(averaged, inverse, decoded)


def solution(mesh):
    placed = (
        P(None, ("groups", "span"), None, ("mp", "seq")),
        P(None, None, ("groups", "span"), None, ("mp", "seq")),
        P(None, ("groups", "span"), None, ("mp", "seq")),
        P("groups", None),
        P("groups", None),
        P(("groups", "span"), None, ("mp", "seq")),
        P(("mp", "seq"), None),
        P(),
        P(("groups", "span")),
    )
    sizes = (mesh.shape["span"], mesh.shape["mp"], mesh.shape["seq"])
    return jax.shard_map(
        functools.partial(per_device, sizes),
        mesh=mesh,
        in_specs=placed,
        out_specs=(
            P(None, ("groups", "span"), None, ("mp", "seq")),
            P(("groups", "span"), ("mp", "seq"), None),
        ),
        check_vma=False,
    )
```

```python
import functools
import math

import jax
import jax.numpy as jnp
from jax import lax
from jax.experimental import pallas as pl
from jax.experimental.pallas import tpu as pltpu
from jax.sharding import PartitionSpec as P

FR = 6
HD = 128
KT = 3
FADE = 2
NSTEPS = 64
LANES = 128
MESH = pl.DeviceIdType.MESH
LOG2E = 1.4426950408889634
LOW = -1e30
F32 = jnp.float32
BF16 = jnp.bfloat16


def nt_dot(a, b):
    return lax.dot_general(a, b, (((1,), (1,)), ((), ())), preferred_element_type=F32)


def tn_dot(a, b):
    return lax.dot_general(a, b, (((0,), (0,)), ((), ())), preferred_element_type=F32)


def head_cols(h):
    return pl.ds(pl.multiple_of(h * HD, HD), HD)


def kernel(
    dims,
    mask_hbm, index_hbm, fade_hbm, query_hbm, noisy_hbm, clean_hbm, fin_hbm, win_hbm, conv_hbm,
    avg_ref, inv_ref, dec_ref,
    q_ref, noisy_ref, fin_ref, win_ref, conv_ref, own_ref, kv_ref, lastq_ref,
    m_ref, l_ref, o_ref, osend_ref, oin_ref, mlsend_ref, mlin_ref,
    part_ref, part_in, hid_ref, prev_ref, sq_ref, stat_in, late_ref, late_in, late_sum, late_got, mask_ref, index_ref, fade_ref,
    load_sem, kv_send, kv_recv, lastq_send, lastq_recv, o_send, o_recv, ml_send, ml_recv,
    part_send, part_recv, hid_send, hid_recv, stat_send, stat_recv,
    late_send, late_recv, back_send, back_recv, sum_send, sum_recv,
):
    n, mp_n, seq_n, steps, ct, heads, rows, rp, main = dims
    group = mp_n * seq_n
    rest = ct - main
    total = steps * ct
    p = lax.axis_index("span")
    g = lax.axis_index("mp") * seq_n + lax.axis_index("seq")
    last, helper = n - 1, n - 2
    feeds = p < helper
    helps = p == helper
    ends = (p == last) & (n > 1)
    blocks = max(helper, 0)
    routed = min(2, heads) if n > 1 else 0
    final = heads - 1 if n > 1 and heads > routed else heads

    def peer(d):
        other = lax.rem(g + d, group)
        return other, {"mp": other // seq_n, "seq": lax.rem(other, seq_n)}

    barrier = pltpu.get_barrier_semaphore()

    @pl.when(p > 0)
    def _():
        pl.semaphore_signal(barrier, inc=1, device_id={"span": p - 1}, device_id_type=MESH)

    @pl.when(p < n - 1)
    def _():
        pl.semaphore_signal(barrier, inc=1, device_id={"span": p + 1}, device_id_type=MESH)

    for d in range(1, group):
        pl.semaphore_signal(barrier, inc=1, device_id=peer(d)[1], device_id_type=MESH)

    near = (p > 0).astype(jnp.int32) + (p < n - 1).astype(jnp.int32)
    loads = []
    for i, (src, dst) in enumerate(
        (
            (fin_hbm, fin_ref), (win_hbm, win_ref), (query_hbm, q_ref), (noisy_hbm, noisy_ref),
            (mask_hbm, mask_ref), (index_hbm, index_ref), (fade_hbm, fade_ref), (conv_hbm, conv_ref),
            (clean_hbm, own_ref),
        )
    ):
        loads.append(pltpu.make_async_copy(src, dst, load_sem.at[i]))
    for copy in loads[:2]:
        copy.start()

    pl.semaphore_wait(barrier, group - 1 + near)

    def kv_copy(src, slot, h):
        return pltpu.make_async_remote_copy(
            src_ref=src, dst_ref=kv_ref.at[slot, h], send_sem=kv_send.at[slot, h],
            recv_sem=kv_recv.at[slot, h], device_id={"span": p + 1}, device_id_type=MESH,
        )

    def own_kv_copy(h):
        return kv_copy(clean_hbm.at[:, 0, :, head_cols(h)], 0, h)

    def lastq_copy(h):
        return pltpu.make_async_remote_copy(
            src_ref=query_hbm.at[:, 0, :, head_cols(h)], dst_ref=lastq_ref.at[h],
            send_sem=lastq_send.at[h], recv_sem=lastq_recv.at[h],
            device_id={"span": p - 1}, device_id_type=MESH,
        )

    def o_copy(h):
        return pltpu.make_async_remote_copy(
            src_ref=osend_ref.at[h], dst_ref=oin_ref.at[h], send_sem=o_send.at[h],
            recv_sem=o_recv.at[h], device_id={"span": p + 1}, device_id_type=MESH,
        )

    def ml_copy(h):
        return pltpu.make_async_remote_copy(
            src_ref=mlsend_ref.at[h], dst_ref=mlin_ref.at[h], send_sem=ml_send.at[h],
            recv_sem=ml_recv.at[h], device_id={"span": p + 1}, device_id_type=MESH,
        )

    def back_copies():
        where = {"span": p - 1}
        return [
            pltpu.make_async_remote_copy(
                src_ref=src.at[final], dst_ref=dst.at[final], send_sem=back_send.at[i],
                recv_sem=back_recv.at[i], device_id=where, device_id_type=MESH,
            )
            for i, (src, dst) in enumerate(((mlsend_ref, mlin_ref), (osend_ref, oin_ref)))
        ]

    def late_copy(d):
        return pltpu.make_async_remote_copy(
            src_ref=late_ref, dst_ref=late_in.at[d - 1], send_sem=late_send.at[d - 1],
            recv_sem=late_recv.at[d - 1], device_id=peer(d)[1], device_id_type=MESH,
        )

    def sum_copy():
        return pltpu.make_async_remote_copy(
            src_ref=late_sum, dst_ref=late_got, send_sem=sum_send, recv_sem=sum_recv,
            device_id={"span": p + 1}, device_id_type=MESH,
        )

    def part_copy(d):
        other, where = peer(d)
        return pltpu.make_async_remote_copy(
            src_ref=part_ref.at[other], dst_ref=part_in.at[d - 1], send_sem=part_send.at[d - 1],
            recv_sem=part_recv.at[d - 1], device_id=where, device_id_type=MESH,
        )

    def stat_copy(d):
        return pltpu.make_async_remote_copy(
            src_ref=sq_ref, dst_ref=stat_in.at[d - 1], send_sem=stat_send.at[d - 1],
            recv_sem=stat_recv.at[d - 1], device_id=peer(d)[1], device_id_type=MESH,
        )

    hid_copy = pltpu.make_async_remote_copy(
        src_ref=hid_ref, dst_ref=prev_ref, send_sem=hid_send, recv_sem=hid_recv,
        device_id={"span": p + 1}, device_id_type=MESH,
    )

    def every_head(body, first=0):
        lax.fori_loop(first, heads, lambda h, c: (body(h), c)[1], 0)

    ahead = max(routed, 1)

    @pl.when(feeds)
    def _():
        for h in range(ahead):
            own_kv_copy(h).start()

    @pl.when(helps)
    def _():
        for h in range(routed):
            own_kv_copy(h).start()

    @pl.when(ends)
    def _():
        every_head(lambda h: lastq_copy(h).start(), routed)

    for copy in loads[2:8]:
        copy.start()

    @pl.when(helps)
    def _():
        loads[8].start()

    def arrive(j, h):
        kv_copy(kv_ref.at[j, h], j, h).wait_recv()

    def hand_on(j, h):
        arrive(j, h)
        kv_copy(kv_ref.at[j, h], j + 1, h).start()

    def pass_on(h):
        lax.fori_loop(0, p, lambda j, c: (hand_on(j, h), c)[1], 0)

        @pl.when((h + 1 >= ahead) & (h + 1 < heads))
        def _():
            own_kv_copy(h + 1).start()

    @pl.when(feeds)
    def _():
        for h in range(ahead):
            pass_on(h)

    loads[0].wait()
    loads[1].wait()
    partial = jnp.dot(fin_ref[0], win_ref[...], preferred_element_type=F32).astype(BF16)
    row = lax.broadcasted_iota(jnp.int32, (rp, ct), 0)
    col = lax.broadcasted_iota(jnp.int32, (rp, ct), 1)
    for o in range(group):
        pick = jnp.where((row < rows) & (col == row + o * rows), 1.0, 0.0).astype(BF16)
        part_ref[o] = jnp.dot(pick, partial, preferred_element_type=F32).astype(BF16)
    for d in range(1, group):
        part_copy(d).start()

    for i in (2, 3, 4, 5, 6):
        loads[i].wait()

    @pl.when(helps)
    def _():
        loads[8].wait()

    lane = lax.broadcasted_iota(jnp.int32, (1, total), 1)
    split = steps * main
    step_of = jnp.zeros((1, total), jnp.int32)
    for s in range(1, steps):
        step_of = step_of + (
            ((lane >= s * main) & (lane < split)) | (lane >= split + s * rest)
        ).astype(jnp.int32)

    def scale_row(segment):
        indices = jnp.zeros((1, total), F32)
        for s in range(steps):
            indices = jnp.where(step_of == s, index_ref[segment, s].astype(F32), indices)
        fraction = 1.0 - indices / NSTEPS
        level = 3.0 * fraction / (1.0 + 2.0 * fraction)
        return (0.5 + level) * (LOG2E / math.sqrt(HD))

    scale = scale_row(p)
    last_scale = scale_row(last)

    whole = [(s, 0, main) for s in range(steps if main else 0)]
    tail = [(s, main, ct) for s in range(steps if rest else 0)]
    tiles = [(0, total, whole + tail)]

    def query_tile(t, row):
        return jnp.concatenate([row(*piece) for piece in tiles[t][2]], 0)

    def own_query(h):
        return lambda s, lo, hi: q_ref[s, 0, lo:hi, head_cols(h)]

    def last_query(h):
        return lambda s, lo, hi: lastq_ref[h, s, lo:hi, :]

    def part_of(ref, tile):
        return ref[:, tile[0] : tile[0] + tile[1]]

    def one_pass(c, scored, old=None):
        tops = []
        for scores, _, visible in scored:
            top = scores.max(0, keepdims=True) * c
            tops.append(top if visible is None else jnp.where(visible > 0, top, LOW))
        m = functools.reduce(jnp.maximum, tops)
        if old is not None:
            m = jnp.maximum(m, old[0])
        l, o, weights, values = 0.0, 0.0, [], []
        for scores, held, visible in scored:
            base = m if visible is None else jnp.where(visible > 0, m, -LOW)
            w = jnp.exp2(scores * c - base)
            l = l + w.sum(0, keepdims=True)
            if callable(held):
                o = o + held(w)
            else:
                weights.append(w.astype(BF16))
                values.append(held)
        if values:
            o = o + tn_dot(jnp.concatenate(values, 0), jnp.concatenate(weights, 0))
        if old is not None:
            factor = jnp.exp2(old[0] - m)
            l = l + old[1] * factor
            o = o + old[2] * factor
        return m, l, o

    def plain(keys, values, queries, visible):
        return nt_dot(keys, queries), values, visible

    def noisy(h, t, queries):
        keys = lambda s: noisy_ref[s, 0, 0, :, head_cols(h)]
        values = lambda s: noisy_ref[s, 1, 0, :, head_cols(h)]
        cut = lambda k: slice(k * main, (k + 1) * main)
        scores = [nt_dot(keys(k), queries[cut(k)]) for k, _, _ in whole]
        if tail:
            owner = lax.broadcasted_iota(jnp.int32, (ct, steps * rest), 1) // rest
            every = nt_dot(jnp.concatenate([keys(s) for s in range(steps)], 0), queries[split:])
            picked = every[0:ct]
            for s in range(1, steps):
                picked = jnp.where(owner == s, every[s * ct : (s + 1) * ct], picked)
            scores.append(picked)

        def weigh(w):
            o = [tn_dot(values(k), w[:, cut(k)].astype(BF16)) for k, _, _ in whole]
            if tail:
                late = w[:, split:]
                mine = [jnp.where(owner == s, late, 0.0).astype(BF16) for s in range(steps)]
                o.append(
                    tn_dot(jnp.concatenate([values(s) for s in range(steps)], 0), jnp.concatenate(mine, 0))
                )
            return jnp.concatenate(o, 1)

        return jnp.concatenate(scores, 1), weigh, None

    def own_state(h):
        for t, tile in enumerate(tiles):
            queries = query_tile(t, own_query(h))
            m, l, o = one_pass(part_of(scale, tile), [noisy(h, t, queries)])
            cols = slice(tile[0], tile[0] + tile[1])
            m_ref[h, :, cols], l_ref[h, :, cols], o_ref[h, :, cols] = m, l, o

    def own_update(j, h):
        visible = mask_ref[p, p - 1 - j]
        for t, tile in enumerate(tiles):
            queries = query_tile(t, own_query(h))
            cols = slice(tile[0], tile[0] + tile[1])
            old = m_ref[h, :, cols], l_ref[h, :, cols], o_ref[h, :, cols]
            block = plain(kv_ref[j, h, 0], kv_ref[j, h, 1], queries, visible)
            m, l, o = one_pass(part_of(scale, tile), [block], old)
            m_ref[h, :, cols], l_ref[h, :, cols], o_ref[h, :, cols] = m, l, o

    def finish_tile(h, t, averaged, count=True):
        lo, width, pieces = tiles[t]
        if count:
            sq_ref[:, lo : lo + width] += jnp.sum(averaged * averaged, 0, keepdims=True)
        turned = jnp.transpose(averaged)
        at = 0
        for s, first, end in pieces:
            avg_ref[s, 0, first:end, head_cols(h)] = turned[at : at + end - first]
            at += end - first

    def finish_own(h):
        for t, tile in enumerate(tiles):
            cols = slice(tile[0], tile[0] + tile[1])
            finish_tile(h, t, o_ref[h, :, cols] * (1.0 / l_ref[h, :, cols]))

    fold = LANES // (steps * rest) if rest else 1

    def pack(h, t, o):
        for i in range(split // LANES):
            osend_ref[h, i * HD : (i + 1) * HD, :] = o[:, i * LANES : (i + 1) * LANES].astype(BF16)
        if rest:
            high, at = HD // fold, split // LANES * HD
            pieces = [o[i * high : (i + 1) * high, split:] for i in range(fold)]
            osend_ref[h, at : at + high, :] = jnp.concatenate(pieces, 1).astype(BF16)

    def unpack(h, t):
        pieces = [
            oin_ref[h, i * HD : (i + 1) * HD, :].astype(F32) for i in range(split // LANES)
        ]
        if rest:
            high, at, width = HD // fold, split // LANES * HD, steps * rest
            held = oin_ref[h, at : at + high, :].astype(F32)
            pieces.append(
                jnp.concatenate([held[:, i * width : (i + 1) * width] for i in range(fold)], 0)
            )
        return jnp.concatenate(pieces, 1)

    def finish_last(h):
        ml_copy(h).wait_recv()
        o_copy(h).wait_recv()
        for t, tile in enumerate(tiles):
            cols = slice(tile[0], tile[0] + tile[1])
            mine, theirs = m_ref[h, :, cols], mlin_ref[h, 0, :, cols]
            m = jnp.maximum(mine, theirs)
            a, b = jnp.exp2(mine - m), jnp.exp2(theirs - m)
            inverse = 1.0 / (l_ref[h, :, cols] * a + mlin_ref[h, 1, :, cols] * b)
            finish_tile(h, t, o_ref[h, :, cols] * (a * inverse) + unpack(h, t) * (b * inverse))

    together = min(blocks, 3)

    def help_sums(h, c, first, queries, segment, old=None):
        def arrived(j):
            visible = mask_ref[segment, helper - 1 - j]
            return plain(kv_ref[j, h, 0], kv_ref[j, h, 1], queries, visible)

        sums = one_pass(c, [first] + [arrived(j) for j in range(together)], old)
        if blocks > together:
            sums = lax.fori_loop(
                together, blocks, lambda j, old: one_pass(c, [arrived(j)], old), sums
            )
        return sums

    def help_last(h, closing=False):
        for t, tile in enumerate(tiles):
            queries = query_tile(t, last_query(h))
            cols = slice(tile[0], tile[0] + tile[1])
            old = None
            if closing:
                old = mlin_ref[h, 0, :, cols], mlin_ref[h, 1, :, cols], unpack(h, t)
            own = plain(
                own_ref[0, 0, :, head_cols(h)], own_ref[1, 0, :, head_cols(h)], queries,
                mask_ref[last, helper],
            )
            m, l, o = help_sums(h, part_of(last_scale, tile), own, queries, last, old)
            if closing:
                o = o * (1.0 / l)
                late_ref[:, cols] = jnp.sum(o * o, 0, keepdims=True)
            else:
                mlsend_ref[h, 0, :, cols], mlsend_ref[h, 1, :, cols] = m, l
            pack(h, t, o)

    def help_own(h):
        for t, tile in enumerate(tiles):
            queries = query_tile(t, own_query(h))
            m, l, o = help_sums(h, part_of(scale, tile), noisy(h, t, queries), queries, helper)
            finish_tile(h, t, o * (1.0 / l))

    def gather_hidden():
        for d in range(1, group):
            part_copy(d).wait()
        summed = part_ref[g].astype(F32)
        for d in range(1, group):
            summed = summed + part_in[d - 1].astype(F32)
        hid_ref[...] = summed.astype(BF16)

    def update_all(h):
        lax.fori_loop(0, p, lambda j, c: (own_update(j, h), c)[1], 0)

    def first_heads(h):
        @pl.when(feeds & (h + ahead < heads))
        def _():
            pass_on(h + ahead)

        @pl.when(jnp.logical_not(helps) & (h == min(1, heads - 1)))
        def _():
            gather_hidden()

        @pl.when(helps)
        def _():
            @pl.when(h >= routed)
            def _():
                lax.fori_loop(0, blocks, lambda j, c: (arrive(j, h), c)[1], 0)
                lastq_copy(h).wait_recv()

            @pl.when((h >= routed) & (h < final))
            def _():
                help_last(h)
                ml_copy(h).start()
                o_copy(h).start()

            if final < heads:

                @pl.when(h == final)
                def _():
                    for copy in back_copies():
                        copy.wait_recv()
                    help_last(final, True)
                    o_copy(final).start()
                    for d in range(1, group):
                        late_copy(d).start()

            help_own(h)

        @pl.when(jnp.logical_not(helps))
        def _():
            own_state(h)

        @pl.when(jnp.logical_not(helps | ends))
        def _():
            update_all(h)
            finish_own(h)

    def last_routed(h):
        lax.fori_loop(0, p, lambda j, c: (arrive(j, h), c)[1], 0)
        update_all(h)
        finish_own(h)

    def decode():
        loads[7].wait()

        @pl.when(p > 0)
        def _():
            hid_copy.wait_recv()

        @pl.when(p == 0)
        def _():
            prev_ref[...] = jnp.zeros_like(prev_ref)

        now = hid_ref[...].astype(F32)
        before = prev_ref[...].astype(F32)
        width = now.shape[1]
        frame = lax.rem(lax.broadcasted_iota(jnp.int32, (rp, width), 0), FR)
        mixed = jnp.zeros((2 * rp, width), F32)
        for k in range(KT):
            late = pltpu.roll(before, k, 0) if k else before
            if k:
                cur = jnp.where(
                    frame >= k, pltpu.roll(now, k, 0), pltpu.roll(before, rp + k - FR, 0)
                )
            else:
                cur = now
            window = jnp.concatenate([cur, late], 0).astype(BF16)
            mixed = mixed + jnp.dot(window, conv_ref[k], preferred_element_type=F32)
        frames = jax.nn.silu(mixed).astype(BF16).astype(F32)
        cur, late = frames[:rp], frames[rp:]
        fade = fade_ref[0]
        aligned = jnp.zeros_like(late)
        for count in range(1, FADE + 1):
            aligned = jnp.where(fade == count, pltpu.roll(late, rp - FR + count, 0), aligned)
        active = (frame < fade) & (p > 0)
        fade_f = fade.astype(F32)
        weight = (frame.astype(F32) + 1.0) / (jnp.zeros((rp, width), F32) + fade_f + 1.0)
        mix = weight * cur + (1.0 - weight) * aligned
        dec_ref[0] = jnp.where(active, mix, cur)[:rows].astype(BF16)

    sq_ref[...] = jnp.zeros_like(sq_ref)

    @pl.when(helps)
    def _():
        def hand_on_routed(j, carry):
            for h in range(routed):
                hand_on(j, h)
            return carry

        lax.fori_loop(0, min(blocks, 1), hand_on_routed, 0)
        gather_hidden()
        hid_copy.start()
        lax.fori_loop(min(blocks, 1), blocks, hand_on_routed, 0)

    every_head(first_heads)

    @pl.when(feeds)
    def _():
        hid_copy.start()

    @pl.when(ends)
    def _():
        if final < heads:
            for t, tile in enumerate(tiles):
                cols = slice(tile[0], tile[0] + tile[1])
                pack(final, t, o_ref[final, :, cols])
            mlsend_ref[final, 0] = m_ref[final]
            mlsend_ref[final, 1] = l_ref[final]
            for copy in back_copies():
                copy.start()

    @pl.when(jnp.logical_not(helps))
    def _():
        decode()

    @pl.when(ends)
    def _():
        for h in range(routed):
            last_routed(h)
        lax.fori_loop(routed, final, lambda h, c: (finish_last(h), c)[1], 0)

    for d in range(1, group):
        stat_copy(d).start()

    @pl.when(helps)
    def _():
        decode()
        if final < heads:
            sums = late_ref[...]
            for d in range(1, group):
                late_copy(d).wait_recv()
                sums = sums + late_in[d - 1]
            late_sum[...] = sums
            sum_copy().start()

    for d in range(1, group):
        stat_copy(d).wait()
    squares = sq_ref[...]
    for d in range(1, group):
        squares = squares + stat_in[d - 1]

    def invert(sums):
        inv_ref[...] = lax.rsqrt(sums / (HD * heads * group) + 1e-06)

    @pl.when(jnp.logical_not(ends))
    def _():
        invert(squares)

    @pl.when(ends)
    def _():
        if final < heads:
            o_copy(final).wait_recv()
            for t in range(len(tiles)):
                finish_tile(final, t, unpack(final, t), False)
            sum_copy().wait_recv()
            invert(squares + late_got[...])
        else:
            invert(squares)

    @pl.when(p < n - 1)
    def _():
        hid_copy.wait_send()

    def drain_kv(h):
        def one(j, carry):
            kv_copy(clean_hbm.at[:, 0, :, head_cols(h)], j, h).wait_send()
            return carry

        lax.fori_loop(0, p + 1, one, 0)

    @pl.when(feeds)
    def _():
        every_head(drain_kv)

    @pl.when(helps)
    def _():
        for h in range(routed):
            drain_kv(h)

        def drain(h):
            ml_copy(h).wait_send()
            o_copy(h).wait_send()

        lax.fori_loop(routed, final, lambda h, c: (drain(h), c)[1], 0)
        if final < heads:
            o_copy(final).wait_send()
            for d in range(1, group):
                late_copy(d).wait_send()
            sum_copy().wait_send()

    @pl.when(ends)
    def _():
        every_head(lambda h: lastq_copy(h).wait_send(), routed)
        if final < heads:
            for copy in back_copies():
                copy.wait_send()


def write_out(dims, avg_ref, inv_ref, dec_ref, att_hbm, dec_hbm, att_ref, sem):
    steps, ct, heads, main = dims
    rest, split = ct - main, steps * main
    dec_copy = pltpu.make_async_copy(dec_ref, dec_hbm, sem.at[steps])
    dec_copy.start()
    inverse = jnp.transpose(jnp.broadcast_to(inv_ref[...], (HD, steps * ct)))
    copies = []
    for s in range(steps):
        spans = [(0, main, s * main)] if main else []
        if rest:
            spans.append((main, ct, split + s * rest))
        for lo, hi, at in spans:
            for h in range(heads):
                cols = slice(h * HD, (h + 1) * HD)
                att_ref[s, 0, lo:hi, cols] = (
                    avg_ref[s, 0, lo:hi, cols] * inverse[at : at + hi - lo]
                ).astype(BF16)
        copy = pltpu.make_async_copy(att_ref.at[s], att_hbm.at[s], sem.at[s])
        copy.start()
        copies.append(copy)
    for copy in copies:
        copy.wait()
    dec_copy.wait()


def per_device(sizes, query, noisy_kv, clean_kv, causal_mask, step_index, finished, w_in, conv_w, fade_count):
    n, mp_n, seq_n = sizes
    group = mp_n * seq_n
    steps, _, ct, width = query.shape
    heads = width // HD
    channels = w_in.shape[1]
    rows = ct // group
    rp = -(-rows // 16) * 16
    main = ct // LANES * LANES
    total = steps * ct
    dims = (n, mp_n, seq_n, steps, ct, heads, rows, rp, main)
    vmem = pltpu.VMEM
    dma = pltpu.SemaphoreType.DMA
    hbm = pl.BlockSpec(memory_space=pltpu.HBM)
    out = pl.BlockSpec(memory_space=pltpu.VMEM)
    slots = max(n - 1, 1)
    arguments = [
        pltpu.with_memory_space_constraint(x, pltpu.HBM)
        for x in (causal_mask, step_index, query, noisy_kv, clean_kv, finished, w_in, conv_w)
    ]
    arguments.insert(2, fade_count)
    averaged, inverse, decoded = pl.pallas_call(
        functools.partial(kernel, dims),
        out_shape=(
            jax.ShapeDtypeStruct(query.shape, F32),
            jax.ShapeDtypeStruct((1, total), F32),
            jax.ShapeDtypeStruct((1, rows, channels), BF16),
        ),
        in_specs=[hbm] * 9,
        out_specs=(out, out, out),
        scratch_shapes=[
            vmem(query.shape, BF16),
            vmem(noisy_kv.shape, BF16),
            vmem(finished.shape, BF16),
            vmem(w_in.shape, BF16),
            vmem(conv_w.shape, BF16),
            vmem(clean_kv.shape, BF16),
            vmem((slots, heads, 2, ct, HD), BF16),
            vmem((heads, steps, ct, HD), BF16),
            vmem((heads, 1, total), F32),
            vmem((heads, 1, total), F32),
            vmem((heads, HD, total), F32),
            vmem((heads, total * HD // LANES, LANES), BF16),
            vmem((heads, total * HD // LANES, LANES), BF16),
            vmem((heads, 2, 1, total), F32),
            vmem((heads, 2, 1, total), F32),
            vmem((group, rp, channels), BF16),
            vmem((group - 1, rp, channels), BF16),
            vmem((rp, channels), BF16),
            vmem((rp, channels), BF16),
            vmem((1, total), F32),
            vmem((group - 1, 1, total), F32),
            vmem((1, total), F32),
            vmem((group - 1, 1, total), F32),
            vmem((1, total), F32),
            vmem((1, total), F32),
            pltpu.SMEM(causal_mask.shape, jnp.int32),
            pltpu.SMEM(step_index.shape, jnp.int32),
            pltpu.SMEM(fade_count.shape, jnp.int32),
            dma((9,)),
            dma((slots, heads)),
            dma((slots, heads)),
            dma((heads,)),
            dma((heads,)),
            dma((heads,)),
            dma((heads,)),
            dma((heads,)),
            dma((heads,)),
            dma((group - 1,)),
            dma((group - 1,)),
            dma,
            dma,
            dma((group - 1,)),
            dma((group - 1,)),
            dma((group - 1,)),
            dma((group - 1,)),
            dma((2,)),
            dma((2,)),
            dma,
            dma,
        ],
        compiler_params=pltpu.CompilerParams(
            collective_id=0, has_side_effects=True, vmem_limit_bytes=28 * 2**20
        ),
    )(*arguments)
    return pl.pallas_call(
        functools.partial(write_out, (steps, ct, heads, main)),
        out_shape=(
            jax.ShapeDtypeStruct(query.shape, BF16),
            jax.ShapeDtypeStruct(decoded.shape, BF16),
        ),
        in_specs=[out] * 3,
        out_specs=(hbm, hbm),
        scratch_shapes=[vmem(query.shape, BF16), dma((steps + 1,))],
        compiler_params=pltpu.CompilerParams(vmem_limit_bytes=8 * 2**20),
    )(averaged, inverse, decoded)


def solution(mesh):
    placed = (
        P(None, ("groups", "span"), None, ("mp", "seq")),
        P(None, None, ("groups", "span"), None, ("mp", "seq")),
        P(None, ("groups", "span"), None, ("mp", "seq")),
        P("groups", None),
        P("groups", None),
        P(("groups", "span"), None, ("mp", "seq")),
        P(("mp", "seq"), None),
        P(),
        P(("groups", "span")),
    )
    sizes = (mesh.shape["span"], mesh.shape["mp"], mesh.shape["seq"])
    return jax.shard_map(
        functools.partial(per_device, sizes),
        mesh=mesh,
        in_specs=placed,
        out_specs=(
            P(None, ("groups", "span"), None, ("mp", "seq")),
            P(("groups", "span"), ("mp", "seq"), None),
        ),
        check_vma=False,
    )
```

```python
import functools
import math

import jax
import jax.numpy as jnp
from jax import lax
from jax.experimental import pallas as pl
from jax.experimental.pallas import tpu as pltpu
from jax.sharding import PartitionSpec as P

FR = 6
HD = 128
KT = 3
FADE = 2
NSTEPS = 64
LANES = 128
MESH = pl.DeviceIdType.MESH
LOG2E = 1.4426950408889634
LOW = -1e30
F32 = jnp.float32
BF16 = jnp.bfloat16


def nt_dot(a, b):
    return lax.dot_general(a, b, (((1,), (1,)), ((), ())), preferred_element_type=F32)


def tn_dot(a, b):
    return lax.dot_general(a, b, (((0,), (0,)), ((), ())), preferred_element_type=F32)


def head_cols(h):
    return pl.ds(pl.multiple_of(h * HD, HD), HD)


def kernel(
    dims,
    mask_hbm, index_hbm, fade_hbm, query_hbm, noisy_hbm, clean_hbm, fin_hbm, win_hbm, conv_hbm,
    avg_ref, inv_ref, dec_ref,
    q_ref, noisy_ref, fin_ref, win_ref, conv_ref, own_ref, kv_ref, lastq_ref,
    m_ref, l_ref, o_ref, osend_ref, oin_ref, mlsend_ref, mlin_ref,
    part_ref, part_in, hid_ref, prev_ref, sq_ref, stat_in, late_ref, late_in, late_sum, late_got, mask_ref, index_ref, fade_ref,
    load_sem, kv_send, kv_recv, lastq_send, lastq_recv, o_send, o_recv, ml_send, ml_recv,
    part_send, part_recv, hid_send, hid_recv, stat_send, stat_recv,
    late_send, late_recv, back_send, back_recv, sum_send, sum_recv,
):
    n, mp_n, seq_n, steps, ct, heads, rows, rp, main = dims
    group = mp_n * seq_n
    rest = ct - main
    total = steps * ct
    p = lax.axis_index("span")
    g = lax.axis_index("mp") * seq_n + lax.axis_index("seq")
    last, helper = n - 1, n - 2
    feeds = p < helper
    helps = p == helper
    ends = (p == last) & (n > 1)
    blocks = max(helper, 0)
    routed = min(2, heads) if n > 1 else 0
    final = heads - 1 if n > 1 and heads > routed else heads

    def peer(d):
        other = lax.rem(g + d, group)
        return other, {"mp": other // seq_n, "seq": lax.rem(other, seq_n)}

    barrier = pltpu.get_barrier_semaphore()

    @pl.when(p > 0)
    def _():
        pl.semaphore_signal(barrier, inc=1, device_id={"span": p - 1}, device_id_type=MESH)

    @pl.when(p < n - 1)
    def _():
        pl.semaphore_signal(barrier, inc=1, device_id={"span": p + 1}, device_id_type=MESH)

    for d in range(1, group):
        pl.semaphore_signal(barrier, inc=1, device_id=peer(d)[1], device_id_type=MESH)

    near = (p > 0).astype(jnp.int32) + (p < n - 1).astype(jnp.int32)
    loads = []
    for i, (src, dst) in enumerate(
        (
            (fin_hbm, fin_ref), (win_hbm, win_ref), (query_hbm, q_ref), (noisy_hbm, noisy_ref),
            (mask_hbm, mask_ref), (index_hbm, index_ref), (fade_hbm, fade_ref), (conv_hbm, conv_ref),
            (clean_hbm, own_ref),
        )
    ):
        loads.append(pltpu.make_async_copy(src, dst, load_sem.at[i]))
    for copy in loads[:2]:
        copy.start()

    pl.semaphore_wait(barrier, group - 1 + near)

    def kv_copy(src, slot, h):
        return pltpu.make_async_remote_copy(
            src_ref=src, dst_ref=kv_ref.at[slot, h], send_sem=kv_send.at[slot, h],
            recv_sem=kv_recv.at[slot, h], device_id={"span": p + 1}, device_id_type=MESH,
        )

    def own_kv_copy(h):
        return kv_copy(clean_hbm.at[:, 0, :, head_cols(h)], 0, h)

    def lastq_copy(h):
        return pltpu.make_async_remote_copy(
            src_ref=query_hbm.at[:, 0, :, head_cols(h)], dst_ref=lastq_ref.at[h],
            send_sem=lastq_send.at[h], recv_sem=lastq_recv.at[h],
            device_id={"span": p - 1}, device_id_type=MESH,
        )

    def o_copy(h):
        return pltpu.make_async_remote_copy(
            src_ref=osend_ref.at[h], dst_ref=oin_ref.at[h], send_sem=o_send.at[h],
            recv_sem=o_recv.at[h], device_id={"span": p + 1}, device_id_type=MESH,
        )

    def ml_copy(h):
        return pltpu.make_async_remote_copy(
            src_ref=mlsend_ref.at[h], dst_ref=mlin_ref.at[h], send_sem=ml_send.at[h],
            recv_sem=ml_recv.at[h], device_id={"span": p + 1}, device_id_type=MESH,
        )

    def back_copies():
        where = {"span": p - 1}
        return [
            pltpu.make_async_remote_copy(
                src_ref=src.at[final], dst_ref=dst.at[final], send_sem=back_send.at[i],
                recv_sem=back_recv.at[i], device_id=where, device_id_type=MESH,
            )
            for i, (src, dst) in enumerate(((mlsend_ref, mlin_ref), (osend_ref, oin_ref)))
        ]

    def late_copy(d):
        return pltpu.make_async_remote_copy(
            src_ref=late_ref, dst_ref=late_in.at[d - 1], send_sem=late_send.at[d - 1],
            recv_sem=late_recv.at[d - 1], device_id=peer(d)[1], device_id_type=MESH,
        )

    def sum_copy():
        return pltpu.make_async_remote_copy(
            src_ref=late_sum, dst_ref=late_got, send_sem=sum_send, recv_sem=sum_recv,
            device_id={"span": p + 1}, device_id_type=MESH,
        )

    def part_copy(d):
        other, where = peer(d)
        return pltpu.make_async_remote_copy(
            src_ref=part_ref.at[other], dst_ref=part_in.at[d - 1], send_sem=part_send.at[d - 1],
            recv_sem=part_recv.at[d - 1], device_id=where, device_id_type=MESH,
        )

    def stat_copy(d):
        return pltpu.make_async_remote_copy(
            src_ref=sq_ref, dst_ref=stat_in.at[d - 1], send_sem=stat_send.at[d - 1],
            recv_sem=stat_recv.at[d - 1], device_id=peer(d)[1], device_id_type=MESH,
        )

    hid_copy = pltpu.make_async_remote_copy(
        src_ref=hid_ref, dst_ref=prev_ref, send_sem=hid_send, recv_sem=hid_recv,
        device_id={"span": p + 1}, device_id_type=MESH,
    )

    def every_head(body, first=0):
        lax.fori_loop(first, heads, lambda h, c: (body(h), c)[1], 0)

    ahead = max(routed, 1)

    @pl.when(feeds)
    def _():
        for h in range(ahead):
            own_kv_copy(h).start()

    @pl.when(helps)
    def _():
        for h in range(routed):
            own_kv_copy(h).start()

    @pl.when(ends)
    def _():
        every_head(lambda h: lastq_copy(h).start(), routed)

    for copy in loads[2:8]:
        copy.start()

    @pl.when(helps)
    def _():
        loads[8].start()

    def arrive(j, h):
        kv_copy(kv_ref.at[j, h], j, h).wait_recv()

    def hand_on(j, h):
        arrive(j, h)
        kv_copy(kv_ref.at[j, h], j + 1, h).start()

    def pass_on(h):
        lax.fori_loop(0, p, lambda j, c: (hand_on(j, h), c)[1], 0)

        @pl.when((h + 1 >= ahead) & (h + 1 < heads))
        def _():
            own_kv_copy(h + 1).start()

    @pl.when(feeds)
    def _():
        for h in range(ahead):
            pass_on(h)

    loads[0].wait()
    loads[1].wait()
    partial = jnp.dot(fin_ref[0], win_ref[...], preferred_element_type=F32).astype(BF16)
    row = lax.broadcasted_iota(jnp.int32, (rp, ct), 0)
    col = lax.broadcasted_iota(jnp.int32, (rp, ct), 1)
    for o in range(group):
        pick = jnp.where((row < rows) & (col == row + o * rows), 1.0, 0.0).astype(BF16)
        part_ref[o] = jnp.dot(pick, partial, preferred_element_type=F32).astype(BF16)
    for d in range(1, group):
        part_copy(d).start()

    for i in (2, 3, 4, 5, 6):
        loads[i].wait()

    @pl.when(helps)
    def _():
        loads[8].wait()

    lane = lax.broadcasted_iota(jnp.int32, (1, total), 1)
    split = steps * main
    step_of = jnp.zeros((1, total), jnp.int32)
    for s in range(1, steps):
        step_of = step_of + (
            ((lane >= s * main) & (lane < split)) | (lane >= split + s * rest)
        ).astype(jnp.int32)

    def scale_row(segment):
        indices = jnp.zeros((1, total), F32)
        for s in range(steps):
            indices = jnp.where(step_of == s, index_ref[segment, s].astype(F32), indices)
        fraction = 1.0 - indices / NSTEPS
        level = 3.0 * fraction / (1.0 + 2.0 * fraction)
        return (0.5 + level) * (LOG2E / math.sqrt(HD))

    scale = scale_row(p)
    last_scale = scale_row(last)

    whole = [(s, 0, main) for s in range(steps if main else 0)]
    tail = [(s, main, ct) for s in range(steps if rest else 0)]
    tiles = [(0, total, whole + tail)]

    def query_tile(t, row):
        return jnp.concatenate([row(*piece) for piece in tiles[t][2]], 0)

    def own_query(h):
        return lambda s, lo, hi: q_ref[s, 0, lo:hi, head_cols(h)]

    def last_query(h):
        return lambda s, lo, hi: lastq_ref[h, s, lo:hi, :]

    def part_of(ref, tile):
        return ref[:, tile[0] : tile[0] + tile[1]]

    def one_pass(c, scored, old=None):
        tops = []
        for scores, _, visible in scored:
            top = scores.max(0, keepdims=True) * c
            tops.append(top if visible is None else jnp.where(visible > 0, top, LOW))
        m = functools.reduce(jnp.maximum, tops)
        if old is not None:
            m = jnp.maximum(m, old[0])
        l, o, weights, values = 0.0, 0.0, [], []
        for scores, held, visible in scored:
            base = m if visible is None else jnp.where(visible > 0, m, -LOW)
            w = jnp.exp2(scores * c - base)
            l = l + w.sum(0, keepdims=True)
            if callable(held):
                o = o + held(w)
            else:
                weights.append(w.astype(BF16))
                values.append(held)
        if values:
            o = o + tn_dot(jnp.concatenate(values, 0), jnp.concatenate(weights, 0))
        if old is not None:
            factor = jnp.exp2(old[0] - m)
            l = l + old[1] * factor
            o = o + old[2] * factor
        return m, l, o

    def plain(keys, values, queries, visible):
        return nt_dot(keys, queries), values, visible

    def noisy(h, t, queries):
        keys = lambda s: noisy_ref[s, 0, 0, :, head_cols(h)]
        values = lambda s: noisy_ref[s, 1, 0, :, head_cols(h)]
        cut = lambda k: slice(k * main, (k + 1) * main)
        scores = [nt_dot(keys(k), queries[cut(k)]) for k, _, _ in whole]
        if tail:
            owner = lax.broadcasted_iota(jnp.int32, (ct, steps * rest), 1) // rest
            every = nt_dot(jnp.concatenate([keys(s) for s in range(steps)], 0), queries[split:])
            picked = every[0:ct]
            for s in range(1, steps):
                picked = jnp.where(owner == s, every[s * ct : (s + 1) * ct], picked)
            scores.append(picked)

        def weigh(w):
            o = [tn_dot(values(k), w[:, cut(k)].astype(BF16)) for k, _, _ in whole]
            if tail:
                late = w[:, split:]
                mine = [jnp.where(owner == s, late, 0.0).astype(BF16) for s in range(steps)]
                o.append(
                    tn_dot(jnp.concatenate([values(s) for s in range(steps)], 0), jnp.concatenate(mine, 0))
                )
            return jnp.concatenate(o, 1)

        return jnp.concatenate(scores, 1), weigh, None

    def own_state(h):
        for t, tile in enumerate(tiles):
            queries = query_tile(t, own_query(h))
            m, l, o = one_pass(part_of(scale, tile), [noisy(h, t, queries)])
            cols = slice(tile[0], tile[0] + tile[1])
            m_ref[h, :, cols], l_ref[h, :, cols], o_ref[h, :, cols] = m, l, o

    def own_update(j, h):
        visible = mask_ref[p, p - 1 - j]
        for t, tile in enumerate(tiles):
            queries = query_tile(t, own_query(h))
            cols = slice(tile[0], tile[0] + tile[1])
            old = m_ref[h, :, cols], l_ref[h, :, cols], o_ref[h, :, cols]
            block = plain(kv_ref[j, h, 0], kv_ref[j, h, 1], queries, visible)
            m, l, o = one_pass(part_of(scale, tile), [block], old)
            m_ref[h, :, cols], l_ref[h, :, cols], o_ref[h, :, cols] = m, l, o

    def finish_tile(h, t, averaged, count=True):
        lo, width, pieces = tiles[t]
        if count:
            sq_ref[:, lo : lo + width] += jnp.sum(averaged * averaged, 0, keepdims=True)
        turned = jnp.transpose(averaged)
        at = 0
        for s, first, end in pieces:
            avg_ref[s, 0, first:end, head_cols(h)] = turned[at : at + end - first]
            at += end - first

    def finish_own(h):
        for t, tile in enumerate(tiles):
            cols = slice(tile[0], tile[0] + tile[1])
            finish_tile(h, t, o_ref[h, :, cols] * (1.0 / l_ref[h, :, cols]))

    fold = LANES // (steps * rest) if rest else 1

    def pack(h, t, o):
        for i in range(split // LANES):
            osend_ref[h, i * HD : (i + 1) * HD, :] = o[:, i * LANES : (i + 1) * LANES].astype(BF16)
        if rest:
            high, at = HD // fold, split // LANES * HD
            pieces = [o[i * high : (i + 1) * high, split:] for i in range(fold)]
            osend_ref[h, at : at + high, :] = jnp.concatenate(pieces, 1).astype(BF16)

    def unpack(h, t):
        pieces = [
            oin_ref[h, i * HD : (i + 1) * HD, :].astype(F32) for i in range(split // LANES)
        ]
        if rest:
            high, at, width = HD // fold, split // LANES * HD, steps * rest
            held = oin_ref[h, at : at + high, :].astype(F32)
            pieces.append(
                jnp.concatenate([held[:, i * width : (i + 1) * width] for i in range(fold)], 0)
            )
        return jnp.concatenate(pieces, 1)

    def finish_last(h):
        ml_copy(h).wait_recv()
        o_copy(h).wait_recv()
        for t, tile in enumerate(tiles):
            cols = slice(tile[0], tile[0] + tile[1])
            mine, theirs = m_ref[h, :, cols], mlin_ref[h, 0, :, cols]
            m = jnp.maximum(mine, theirs)
            a, b = jnp.exp2(mine - m), jnp.exp2(theirs - m)
            inverse = 1.0 / (l_ref[h, :, cols] * a + mlin_ref[h, 1, :, cols] * b)
            finish_tile(h, t, o_ref[h, :, cols] * (a * inverse) + unpack(h, t) * (b * inverse))

    def arrived(h, j, queries, segment):
        visible = mask_ref[segment, helper - 1 - j]
        return plain(kv_ref[j, h, 0], kv_ref[j, h, 1], queries, visible)

    def help_sums(h, c, first, queries, segment, count, old=None):
        together = min(count, 3)
        held = [first] + [arrived(h, j, queries, segment) for j in range(together)]
        sums = one_pass(c, held, old)
        if count > together:
            sums = lax.fori_loop(
                together, count,
                lambda j, so_far: one_pass(c, [arrived(h, j, queries, segment)], so_far), sums,
            )
        return sums

    def help_last(h, closing=False):
        early = max(blocks - 1, 0)
        lax.fori_loop(0, early, lambda j, c: (arrive(j, h), c)[1], 0)
        for t, tile in enumerate(tiles):
            queries = query_tile(t, last_query(h))
            cols = slice(tile[0], tile[0] + tile[1])
            old = None
            if closing:
                old = mlin_ref[h, 0, :, cols], mlin_ref[h, 1, :, cols], unpack(h, t)
            own = plain(
                own_ref[0, 0, :, head_cols(h)], own_ref[1, 0, :, head_cols(h)], queries,
                mask_ref[last, helper],
            )
            m, l, o = help_sums(h, part_of(last_scale, tile), own, queries, last, early, old)
            m_ref[h, :, cols], l_ref[h, :, cols], o_ref[h, :, cols] = m, l, o
        if blocks:
            arrive(blocks - 1, h)
        for t, tile in enumerate(tiles):
            queries = query_tile(t, last_query(h))
            cols = slice(tile[0], tile[0] + tile[1])
            m, l, o = m_ref[h, :, cols], l_ref[h, :, cols], o_ref[h, :, cols]
            if blocks:
                block = arrived(h, blocks - 1, queries, last)
                m, l, o = one_pass(part_of(last_scale, tile), [block], (m, l, o))
            if closing:
                o = o * (1.0 / l)
                late_ref[:, cols] = jnp.sum(o * o, 0, keepdims=True)
            else:
                mlsend_ref[h, 0, :, cols], mlsend_ref[h, 1, :, cols] = m, l
            pack(h, t, o)

    def help_own(h):
        for t, tile in enumerate(tiles):
            queries = query_tile(t, own_query(h))
            first = noisy(h, t, queries)
            m, l, o = help_sums(h, part_of(scale, tile), first, queries, helper, blocks)
            finish_tile(h, t, o * (1.0 / l))

    def gather_hidden():
        for d in range(1, group):
            part_copy(d).wait()
        summed = part_ref[g].astype(F32)
        for d in range(1, group):
            summed = summed + part_in[d - 1].astype(F32)
        hid_ref[...] = summed.astype(BF16)

    def update_all(h):
        lax.fori_loop(0, p, lambda j, c: (own_update(j, h), c)[1], 0)

    def first_heads(h):
        @pl.when(feeds & (h + ahead < heads))
        def _():
            pass_on(h + ahead)

        @pl.when(jnp.logical_not(helps) & (h == min(1, heads - 1)))
        def _():
            gather_hidden()

        @pl.when(helps)
        def _():
            @pl.when(h >= routed)
            def _():
                lastq_copy(h).wait_recv()

            @pl.when((h >= routed) & (h < final))
            def _():
                help_last(h)
                ml_copy(h).start()
                o_copy(h).start()

            if final < heads:

                @pl.when(h == final)
                def _():
                    for copy in back_copies():
                        copy.wait_recv()
                    help_last(final, True)
                    o_copy(final).start()
                    for d in range(1, group):
                        late_copy(d).start()

            help_own(h)

        @pl.when(jnp.logical_not(helps))
        def _():
            own_state(h)

        @pl.when(jnp.logical_not(helps | ends))
        def _():
            update_all(h)
            finish_own(h)

    def last_routed(h):
        lax.fori_loop(0, p, lambda j, c: (arrive(j, h), c)[1], 0)
        update_all(h)
        finish_own(h)

    def decode():
        loads[7].wait()

        @pl.when(p > 0)
        def _():
            hid_copy.wait_recv()

        @pl.when(p == 0)
        def _():
            prev_ref[...] = jnp.zeros_like(prev_ref)

        now = hid_ref[...].astype(F32)
        before = prev_ref[...].astype(F32)
        width = now.shape[1]
        frame = lax.rem(lax.broadcasted_iota(jnp.int32, (rp, width), 0), FR)
        mixed = jnp.zeros((2 * rp, width), F32)
        for k in range(KT):
            late = pltpu.roll(before, k, 0) if k else before
            if k:
                cur = jnp.where(
                    frame >= k, pltpu.roll(now, k, 0), pltpu.roll(before, rp + k - FR, 0)
                )
            else:
                cur = now
            window = jnp.concatenate([cur, late], 0).astype(BF16)
            mixed = mixed + jnp.dot(window, conv_ref[k], preferred_element_type=F32)
        frames = jax.nn.silu(mixed).astype(BF16).astype(F32)
        cur, late = frames[:rp], frames[rp:]
        fade = fade_ref[0]
        aligned = jnp.zeros_like(late)
        for count in range(1, FADE + 1):
            aligned = jnp.where(fade == count, pltpu.roll(late, rp - FR + count, 0), aligned)
        active = (frame < fade) & (p > 0)
        fade_f = fade.astype(F32)
        weight = (frame.astype(F32) + 1.0) / (jnp.zeros((rp, width), F32) + fade_f + 1.0)
        mix = weight * cur + (1.0 - weight) * aligned
        dec_ref[0] = jnp.where(active, mix, cur)[:rows].astype(BF16)

    sq_ref[...] = jnp.zeros_like(sq_ref)

    @pl.when(helps)
    def _():
        def hand_on_routed(j, carry):
            for h in range(routed):
                hand_on(j, h)
            return carry

        lax.fori_loop(0, min(blocks, 1), hand_on_routed, 0)
        gather_hidden()
        hid_copy.start()
        lax.fori_loop(min(blocks, 1), blocks, hand_on_routed, 0)

    every_head(first_heads)

    @pl.when(feeds)
    def _():
        hid_copy.start()

    @pl.when(ends)
    def _():
        if final < heads:
            for t, tile in enumerate(tiles):
                cols = slice(tile[0], tile[0] + tile[1])
                pack(final, t, o_ref[final, :, cols])
            mlsend_ref[final, 0] = m_ref[final]
            mlsend_ref[final, 1] = l_ref[final]
            for copy in back_copies():
                copy.start()

    @pl.when(jnp.logical_not(helps))
    def _():
        decode()

    @pl.when(ends)
    def _():
        for h in range(routed):
            last_routed(h)
        lax.fori_loop(routed, final, lambda h, c: (finish_last(h), c)[1], 0)

    for d in range(1, group):
        stat_copy(d).start()

    @pl.when(helps)
    def _():
        decode()
        if final < heads:
            sums = late_ref[...]
            for d in range(1, group):
                late_copy(d).wait_recv()
                sums = sums + late_in[d - 1]
            late_sum[...] = sums
            sum_copy().start()

    if final < heads:

        @pl.when(ends)
        def _():
            o_copy(final).wait_recv()
            for t in range(len(tiles)):
                finish_tile(final, t, unpack(final, t), False)

    for d in range(1, group):
        stat_copy(d).wait_recv()
    squares = sq_ref[...]
    for d in range(1, group):
        squares = squares + stat_in[d - 1]

    def invert(sums):
        inv_ref[...] = lax.rsqrt(sums / (HD * heads * group) + 1e-06)

    @pl.when(jnp.logical_not(ends))
    def _():
        invert(squares)

    @pl.when(ends)
    def _():
        if final < heads:
            sum_copy().wait_recv()
            invert(squares + late_got[...])
        else:
            invert(squares)

    for d in range(1, group):
        stat_copy(d).wait_send()

    @pl.when(p < n - 1)
    def _():
        hid_copy.wait_send()

    def drain_kv(h):
        def one(j, carry):
            kv_copy(clean_hbm.at[:, 0, :, head_cols(h)], j, h).wait_send()
            return carry

        lax.fori_loop(0, p + 1, one, 0)

    @pl.when(feeds)
    def _():
        every_head(drain_kv)

    @pl.when(helps)
    def _():
        for h in range(routed):
            drain_kv(h)

        def drain(h):
            ml_copy(h).wait_send()
            o_copy(h).wait_send()

        lax.fori_loop(routed, final, lambda h, c: (drain(h), c)[1], 0)
        if final < heads:
            o_copy(final).wait_send()
            for d in range(1, group):
                late_copy(d).wait_send()
            sum_copy().wait_send()

    @pl.when(ends)
    def _():
        every_head(lambda h: lastq_copy(h).wait_send(), routed)
        if final < heads:
            for copy in back_copies():
                copy.wait_send()


def write_out(dims, avg_ref, inv_ref, dec_ref, att_hbm, dec_hbm, att_ref, sem):
    steps, ct, heads, main = dims
    rest, split = ct - main, steps * main
    dec_copy = pltpu.make_async_copy(dec_ref, dec_hbm, sem.at[steps])
    dec_copy.start()
    turned = lambda lo, hi: jnp.transpose(jnp.broadcast_to(inv_ref[:, lo:hi], (HD, hi - lo)))
    late = turned(split, steps * ct) if rest else None
    copies = []
    for s in range(steps):
        inverse = turned(s * main, (s + 1) * main) if main else None
        spans = [(0, main, s * main)] if main else []
        if rest:
            spans.append((main, ct, split + s * rest))
        for lo, hi, at in spans:
            for h in range(heads):
                cols = slice(h * HD, (h + 1) * HD)
                att_ref[s, 0, lo:hi, cols] = (
                    avg_ref[s, 0, lo:hi, cols] * (late[at - split : at - split + hi - lo] if lo else inverse)
                ).astype(BF16)
        copy = pltpu.make_async_copy(att_ref.at[s], att_hbm.at[s], sem.at[s])
        copy.start()
        copies.append(copy)
    for copy in copies:
        copy.wait()
    dec_copy.wait()


def per_device(sizes, query, noisy_kv, clean_kv, causal_mask, step_index, finished, w_in, conv_w, fade_count):
    n, mp_n, seq_n = sizes
    group = mp_n * seq_n
    steps, _, ct, width = query.shape
    heads = width // HD
    channels = w_in.shape[1]
    rows = ct // group
    rp = -(-rows // 16) * 16
    main = ct // LANES * LANES
    total = steps * ct
    dims = (n, mp_n, seq_n, steps, ct, heads, rows, rp, main)
    vmem = pltpu.VMEM
    dma = pltpu.SemaphoreType.DMA
    hbm = pl.BlockSpec(memory_space=pltpu.HBM)
    out = pl.BlockSpec(memory_space=pltpu.VMEM)
    slots = max(n - 1, 1)
    arguments = [
        pltpu.with_memory_space_constraint(x, pltpu.HBM)
        for x in (causal_mask, step_index, query, noisy_kv, clean_kv, finished, w_in, conv_w)
    ]
    arguments.insert(2, fade_count)
    averaged, inverse, decoded = pl.pallas_call(
        functools.partial(kernel, dims),
        out_shape=(
            jax.ShapeDtypeStruct(query.shape, F32),
            jax.ShapeDtypeStruct((1, total), F32),
            jax.ShapeDtypeStruct((1, rows, channels), BF16),
        ),
        in_specs=[hbm] * 9,
        out_specs=(out, out, out),
        scratch_shapes=[
            vmem(query.shape, BF16),
            vmem(noisy_kv.shape, BF16),
            vmem(finished.shape, BF16),
            vmem(w_in.shape, BF16),
            vmem(conv_w.shape, BF16),
            vmem(clean_kv.shape, BF16),
            vmem((slots, heads, 2, ct, HD), BF16),
            vmem((heads, steps, ct, HD), BF16),
            vmem((heads, 1, total), F32),
            vmem((heads, 1, total), F32),
            vmem((heads, HD, total), F32),
            vmem((heads, total * HD // LANES, LANES), BF16),
            vmem((heads, total * HD // LANES, LANES), BF16),
            vmem((heads, 2, 1, total), F32),
            vmem((heads, 2, 1, total), F32),
            vmem((group, rp, channels), BF16),
            vmem((group - 1, rp, channels), BF16),
            vmem((rp, channels), BF16),
            vmem((rp, channels), BF16),
            vmem((1, total), F32),
            vmem((group - 1, 1, total), F32),
            vmem((1, total), F32),
            vmem((group - 1, 1, total), F32),
            vmem((1, total), F32),
            vmem((1, total), F32),
            pltpu.SMEM(causal_mask.shape, jnp.int32),
            pltpu.SMEM(step_index.shape, jnp.int32),
            pltpu.SMEM(fade_count.shape, jnp.int32),
            dma((9,)),
            dma((slots, heads)),
            dma((slots, heads)),
            dma((heads,)),
            dma((heads,)),
            dma((heads,)),
            dma((heads,)),
            dma((heads,)),
            dma((heads,)),
            dma((group - 1,)),
            dma((group - 1,)),
            dma,
            dma,
            dma((group - 1,)),
            dma((group - 1,)),
            dma((group - 1,)),
            dma((group - 1,)),
            dma((2,)),
            dma((2,)),
            dma,
            dma,
        ],
        compiler_params=pltpu.CompilerParams(
            collective_id=0, has_side_effects=True, vmem_limit_bytes=28 * 2**20
        ),
    )(*arguments)
    return pl.pallas_call(
        functools.partial(write_out, (steps, ct, heads, main)),
        out_shape=(
            jax.ShapeDtypeStruct(query.shape, BF16),
            jax.ShapeDtypeStruct(decoded.shape, BF16),
        ),
        in_specs=[out] * 3,
        out_specs=(hbm, hbm),
        scratch_shapes=[vmem(query.shape, BF16), dma((steps + 1,))],
        compiler_params=pltpu.CompilerParams(vmem_limit_bytes=8 * 2**20),
    )(averaged, inverse, decoded)


def solution(mesh):
    placed = (
        P(None, ("groups", "span"), None, ("mp", "seq")),
        P(None, None, ("groups", "span"), None, ("mp", "seq")),
        P(None, ("groups", "span"), None, ("mp", "seq")),
        P("groups", None),
        P("groups", None),
        P(("groups", "span"), None, ("mp", "seq")),
        P(("mp", "seq"), None),
        P(),
        P(("groups", "span")),
    )
    sizes = (mesh.shape["span"], mesh.shape["mp"], mesh.shape["seq"])
    return jax.shard_map(
        functools.partial(per_device, sizes),
        mesh=mesh,
        in_specs=placed,
        out_specs=(
            P(None, ("groups", "span"), None, ("mp", "seq")),
            P(("groups", "span"), ("mp", "seq"), None),
        ),
        check_vma=False,
    )
```

```python
import functools
import math

import jax
import jax.numpy as jnp
from jax import lax
from jax.experimental import pallas as pl
from jax.experimental.pallas import tpu as pltpu
from jax.sharding import PartitionSpec as P

FR = 6
HD = 128
KT = 3
FADE = 2
NSTEPS = 64
LANES = 128
MESH = pl.DeviceIdType.MESH
LOG2E = 1.4426950408889634
LOW = -1e30
F32 = jnp.float32
BF16 = jnp.bfloat16


def nt_dot(a, b):
    return lax.dot_general(a, b, (((1,), (1,)), ((), ())), preferred_element_type=F32)


def tn_dot(a, b):
    return lax.dot_general(a, b, (((0,), (0,)), ((), ())), preferred_element_type=F32)


def head_cols(h):
    return pl.ds(pl.multiple_of(h * HD, HD), HD)


def kernel(
    dims,
    mask_hbm, index_hbm, fade_hbm, query_hbm, noisy_hbm, clean_hbm, fin_hbm, win_hbm, conv_hbm,
    avg_ref, inv_ref, dec_ref,
    q_ref, noisy_ref, fin_ref, win_ref, conv_ref, own_ref, kv_ref, lastq_ref,
    m_ref, l_ref, o_ref, osend_ref, oin_ref, mlsend_ref, mlin_ref,
    part_ref, part_in, hid_ref, prev_ref, sq_ref, stat_in, late_ref, late_in, late_sum, late_got, mask_ref, index_ref, fade_ref,
    load_sem, kv_send, kv_recv, lastq_send, lastq_recv, o_send, o_recv, ml_send, ml_recv,
    part_send, part_recv, hid_send, hid_recv, stat_send, stat_recv,
    late_send, late_recv, back_send, back_recv, sum_send, sum_recv,
):
    n, mp_n, seq_n, steps, ct, heads, rows, rp, main = dims
    group = mp_n * seq_n
    rest = ct - main
    total = steps * ct
    p = lax.axis_index("span")
    g = lax.axis_index("mp") * seq_n + lax.axis_index("seq")
    last, helper = n - 1, n - 2
    feeds = p < helper
    helps = p == helper
    ends = (p == last) & (n > 1)
    blocks = max(helper, 0)
    routed = min(2, heads) if n > 1 else 0
    final = max(routed, heads - 2) if n > 1 else heads

    def peer(d):
        other = lax.rem(g + d, group)
        return other, {"mp": other // seq_n, "seq": lax.rem(other, seq_n)}

    barrier = pltpu.get_barrier_semaphore()

    @pl.when(p > 0)
    def _():
        pl.semaphore_signal(barrier, inc=1, device_id={"span": p - 1}, device_id_type=MESH)

    @pl.when(p < n - 1)
    def _():
        pl.semaphore_signal(barrier, inc=1, device_id={"span": p + 1}, device_id_type=MESH)

    for d in range(1, group):
        pl.semaphore_signal(barrier, inc=1, device_id=peer(d)[1], device_id_type=MESH)

    near = (p > 0).astype(jnp.int32) + (p < n - 1).astype(jnp.int32)
    loads = []
    for i, (src, dst) in enumerate(
        (
            (fin_hbm, fin_ref), (win_hbm, win_ref), (query_hbm, q_ref), (noisy_hbm, noisy_ref),
            (mask_hbm, mask_ref), (index_hbm, index_ref), (fade_hbm, fade_ref), (conv_hbm, conv_ref),
            (clean_hbm, own_ref),
        )
    ):
        loads.append(pltpu.make_async_copy(src, dst, load_sem.at[i]))
    for copy in loads[:2]:
        copy.start()

    pl.semaphore_wait(barrier, group - 1 + near)

    def kv_copy(src, slot, h):
        return pltpu.make_async_remote_copy(
            src_ref=src, dst_ref=kv_ref.at[slot, h], send_sem=kv_send.at[slot, h],
            recv_sem=kv_recv.at[slot, h], device_id={"span": p + 1}, device_id_type=MESH,
        )

    def own_kv_copy(h):
        return kv_copy(clean_hbm.at[:, 0, :, head_cols(h)], 0, h)

    def lastq_copy(h):
        return pltpu.make_async_remote_copy(
            src_ref=query_hbm.at[:, 0, :, head_cols(h)], dst_ref=lastq_ref.at[h],
            send_sem=lastq_send.at[h], recv_sem=lastq_recv.at[h],
            device_id={"span": p - 1}, device_id_type=MESH,
        )

    def o_copy(h):
        return pltpu.make_async_remote_copy(
            src_ref=osend_ref.at[h], dst_ref=oin_ref.at[h], send_sem=o_send.at[h],
            recv_sem=o_recv.at[h], device_id={"span": p + 1}, device_id_type=MESH,
        )

    def ml_copy(h):
        return pltpu.make_async_remote_copy(
            src_ref=mlsend_ref.at[h], dst_ref=mlin_ref.at[h], send_sem=ml_send.at[h],
            recv_sem=ml_recv.at[h], device_id={"span": p + 1}, device_id_type=MESH,
        )

    def back_copies(h):
        where = {"span": p - 1}
        return [
            pltpu.make_async_remote_copy(
                src_ref=src.at[h], dst_ref=dst.at[h], send_sem=back_send.at[i, h],
                recv_sem=back_recv.at[i, h], device_id=where, device_id_type=MESH,
            )
            for i, (src, dst) in enumerate(((mlsend_ref, mlin_ref), (osend_ref, oin_ref)))
        ]

    def late_copy(d):
        return pltpu.make_async_remote_copy(
            src_ref=late_ref, dst_ref=late_in.at[d - 1], send_sem=late_send.at[d - 1],
            recv_sem=late_recv.at[d - 1], device_id=peer(d)[1], device_id_type=MESH,
        )

    def sum_copy():
        return pltpu.make_async_remote_copy(
            src_ref=late_sum, dst_ref=late_got, send_sem=sum_send, recv_sem=sum_recv,
            device_id={"span": p + 1}, device_id_type=MESH,
        )

    def part_copy(d):
        other, where = peer(d)
        return pltpu.make_async_remote_copy(
            src_ref=part_ref.at[other], dst_ref=part_in.at[d - 1], send_sem=part_send.at[d - 1],
            recv_sem=part_recv.at[d - 1], device_id=where, device_id_type=MESH,
        )

    def stat_copy(d):
        return pltpu.make_async_remote_copy(
            src_ref=sq_ref, dst_ref=stat_in.at[d - 1], send_sem=stat_send.at[d - 1],
            recv_sem=stat_recv.at[d - 1], device_id=peer(d)[1], device_id_type=MESH,
        )

    hid_copy = pltpu.make_async_remote_copy(
        src_ref=hid_ref, dst_ref=prev_ref, send_sem=hid_send, recv_sem=hid_recv,
        device_id={"span": p + 1}, device_id_type=MESH,
    )

    def every_head(body, first=0):
        lax.fori_loop(first, heads, lambda h, c: (body(h), c)[1], 0)

    ahead = max(routed, 1)

    @pl.when(feeds)
    def _():
        for h in range(ahead):
            own_kv_copy(h).start()

    @pl.when(helps)
    def _():
        for h in range(routed):
            own_kv_copy(h).start()

    @pl.when(ends)
    def _():
        every_head(lambda h: lastq_copy(h).start(), routed)

    for copy in loads[2:8]:
        copy.start()

    @pl.when(helps)
    def _():
        loads[8].start()

    def arrive(j, h):
        kv_copy(kv_ref.at[j, h], j, h).wait_recv()

    def hand_on(j, h):
        arrive(j, h)
        kv_copy(kv_ref.at[j, h], j + 1, h).start()

    def pass_on(h):
        lax.fori_loop(0, p, lambda j, c: (hand_on(j, h), c)[1], 0)

        @pl.when((h + 1 >= ahead) & (h + 1 < heads))
        def _():
            own_kv_copy(h + 1).start()

    @pl.when(feeds)
    def _():
        for h in range(ahead):
            pass_on(h)

    loads[0].wait()
    loads[1].wait()
    partial = jnp.dot(fin_ref[0], win_ref[...], preferred_element_type=F32).astype(BF16)
    row = lax.broadcasted_iota(jnp.int32, (rp, ct), 0)
    col = lax.broadcasted_iota(jnp.int32, (rp, ct), 1)
    for o in range(group):
        pick = jnp.where((row < rows) & (col == row + o * rows), 1.0, 0.0).astype(BF16)
        part_ref[o] = jnp.dot(pick, partial, preferred_element_type=F32).astype(BF16)
    for d in range(1, group):
        part_copy(d).start()

    for i in (2, 3, 4, 5, 6):
        loads[i].wait()

    @pl.when(helps)
    def _():
        loads[8].wait()

    lane = lax.broadcasted_iota(jnp.int32, (1, total), 1)
    split = steps * main
    step_of = jnp.zeros((1, total), jnp.int32)
    for s in range(1, steps):
        step_of = step_of + (
            ((lane >= s * main) & (lane < split)) | (lane >= split + s * rest)
        ).astype(jnp.int32)

    def scale_row(segment):
        indices = jnp.zeros((1, total), F32)
        for s in range(steps):
            indices = jnp.where(step_of == s, index_ref[segment, s].astype(F32), indices)
        fraction = 1.0 - indices / NSTEPS
        level = 3.0 * fraction / (1.0 + 2.0 * fraction)
        return (0.5 + level) * (LOG2E / math.sqrt(HD))

    scale = scale_row(p)
    last_scale = scale_row(last)

    whole = [(s, 0, main) for s in range(steps if main else 0)]
    tail = [(s, main, ct) for s in range(steps if rest else 0)]
    tiles = [(0, total, whole + tail)]

    def query_tile(t, row):
        return jnp.concatenate([row(*piece) for piece in tiles[t][2]], 0)

    def own_query(h):
        return lambda s, lo, hi: q_ref[s, 0, lo:hi, head_cols(h)]

    def last_query(h):
        return lambda s, lo, hi: lastq_ref[h, s, lo:hi, :]

    def part_of(ref, tile):
        return ref[:, tile[0] : tile[0] + tile[1]]

    def one_pass(c, scored, old=None):
        tops = []
        for scores, _, visible in scored:
            top = scores.max(0, keepdims=True) * c
            tops.append(top if visible is None else jnp.where(visible > 0, top, LOW))
        m = functools.reduce(jnp.maximum, tops)
        if old is not None:
            m = jnp.maximum(m, old[0])
        l, o, weights, values = 0.0, 0.0, [], []
        for scores, held, visible in scored:
            base = m if visible is None else jnp.where(visible > 0, m, -LOW)
            w = jnp.exp2(scores * c - base)
            l = l + w.sum(0, keepdims=True)
            if callable(held):
                o = o + held(w)
            else:
                weights.append(w.astype(BF16))
                values.append(held)
        if values:
            o = o + tn_dot(jnp.concatenate(values, 0), jnp.concatenate(weights, 0))
        if old is not None:
            factor = jnp.exp2(old[0] - m)
            l = l + old[1] * factor
            o = o + old[2] * factor
        return m, l, o

    def plain(keys, values, queries, visible):
        return nt_dot(keys, queries), values, visible

    def noisy(h, t, queries):
        keys = lambda s: noisy_ref[s, 0, 0, :, head_cols(h)]
        values = lambda s: noisy_ref[s, 1, 0, :, head_cols(h)]
        cut = lambda k: slice(k * main, (k + 1) * main)
        scores = [nt_dot(keys(k), queries[cut(k)]) for k, _, _ in whole]
        if tail:
            owner = lax.broadcasted_iota(jnp.int32, (ct, steps * rest), 1) // rest
            every = nt_dot(jnp.concatenate([keys(s) for s in range(steps)], 0), queries[split:])
            picked = every[0:ct]
            for s in range(1, steps):
                picked = jnp.where(owner == s, every[s * ct : (s + 1) * ct], picked)
            scores.append(picked)

        def weigh(w):
            o = [tn_dot(values(k), w[:, cut(k)].astype(BF16)) for k, _, _ in whole]
            if tail:
                late = w[:, split:]
                mine = [jnp.where(owner == s, late, 0.0).astype(BF16) for s in range(steps)]
                o.append(
                    tn_dot(jnp.concatenate([values(s) for s in range(steps)], 0), jnp.concatenate(mine, 0))
                )
            return jnp.concatenate(o, 1)

        return jnp.concatenate(scores, 1), weigh, None

    def own_state(h):
        for t, tile in enumerate(tiles):
            queries = query_tile(t, own_query(h))
            m, l, o = one_pass(part_of(scale, tile), [noisy(h, t, queries)])
            cols = slice(tile[0], tile[0] + tile[1])
            m_ref[h, :, cols], l_ref[h, :, cols], o_ref[h, :, cols] = m, l, o

    def own_update(j, h):
        visible = mask_ref[p, p - 1 - j]
        for t, tile in enumerate(tiles):
            queries = query_tile(t, own_query(h))
            cols = slice(tile[0], tile[0] + tile[1])
            old = m_ref[h, :, cols], l_ref[h, :, cols], o_ref[h, :, cols]
            block = plain(kv_ref[j, h, 0], kv_ref[j, h, 1], queries, visible)
            m, l, o = one_pass(part_of(scale, tile), [block], old)
            m_ref[h, :, cols], l_ref[h, :, cols], o_ref[h, :, cols] = m, l, o

    def finish_tile(h, t, averaged, count=True):
        lo, width, pieces = tiles[t]
        if count:
            sq_ref[:, lo : lo + width] += jnp.sum(averaged * averaged, 0, keepdims=True)
        turned = jnp.transpose(averaged)
        at = 0
        for s, first, end in pieces:
            avg_ref[s, 0, first:end, head_cols(h)] = turned[at : at + end - first]
            at += end - first

    def finish_own(h):
        for t, tile in enumerate(tiles):
            cols = slice(tile[0], tile[0] + tile[1])
            finish_tile(h, t, o_ref[h, :, cols] * (1.0 / l_ref[h, :, cols]))

    fold = LANES // (steps * rest) if rest else 1

    def pack(h, t, o):
        for i in range(split // LANES):
            osend_ref[h, i * HD : (i + 1) * HD, :] = o[:, i * LANES : (i + 1) * LANES].astype(BF16)
        if rest:
            high, at = HD // fold, split // LANES * HD
            pieces = [o[i * high : (i + 1) * high, split:] for i in range(fold)]
            osend_ref[h, at : at + high, :] = jnp.concatenate(pieces, 1).astype(BF16)

    def unpack(h, t):
        pieces = [
            oin_ref[h, i * HD : (i + 1) * HD, :].astype(F32) for i in range(split // LANES)
        ]
        if rest:
            high, at, width = HD // fold, split // LANES * HD, steps * rest
            held = oin_ref[h, at : at + high, :].astype(F32)
            pieces.append(
                jnp.concatenate([held[:, i * width : (i + 1) * width] for i in range(fold)], 0)
            )
        return jnp.concatenate(pieces, 1)

    def finish_last(h):
        ml_copy(h).wait_recv()
        o_copy(h).wait_recv()
        for t, tile in enumerate(tiles):
            cols = slice(tile[0], tile[0] + tile[1])
            mine, theirs = m_ref[h, :, cols], mlin_ref[h, 0, :, cols]
            m = jnp.maximum(mine, theirs)
            a, b = jnp.exp2(mine - m), jnp.exp2(theirs - m)
            inverse = 1.0 / (l_ref[h, :, cols] * a + mlin_ref[h, 1, :, cols] * b)
            finish_tile(h, t, o_ref[h, :, cols] * (a * inverse) + unpack(h, t) * (b * inverse))

    def arrived(h, j, queries, segment):
        visible = mask_ref[segment, helper - 1 - j]
        return plain(kv_ref[j, h, 0], kv_ref[j, h, 1], queries, visible)

    def help_sums(h, c, first, queries, segment, count):
        together = min(count, 3)
        held = [first] + [arrived(h, j, queries, segment) for j in range(together)]
        sums = one_pass(c, held)
        if count > together:
            sums = lax.fori_loop(
                together, count,
                lambda j, so_far: one_pass(c, [arrived(h, j, queries, segment)], so_far), sums,
            )
        return sums

    def help_last(h, closing=False):
        early = max(blocks - 1, 0)
        lax.fori_loop(0, early, lambda j, c: (arrive(j, h), c)[1], 0)
        for t, tile in enumerate(tiles):
            queries = query_tile(t, last_query(h))
            cols = slice(tile[0], tile[0] + tile[1])
            own = plain(
                own_ref[0, 0, :, head_cols(h)], own_ref[1, 0, :, head_cols(h)], queries,
                mask_ref[last, helper],
            )
            m, l, o = help_sums(h, part_of(last_scale, tile), own, queries, last, early)
            m_ref[h, :, cols], l_ref[h, :, cols], o_ref[h, :, cols] = m, l, o
        if blocks:
            arrive(blocks - 1, h)
        if closing:
            for copy in back_copies(h):
                copy.wait_recv()
        for t, tile in enumerate(tiles):
            queries = query_tile(t, last_query(h))
            cols = slice(tile[0], tile[0] + tile[1])
            m, l, o = m_ref[h, :, cols], l_ref[h, :, cols], o_ref[h, :, cols]
            if blocks:
                block = arrived(h, blocks - 1, queries, last)
                m, l, o = one_pass(part_of(last_scale, tile), [block], (m, l, o))
            if closing:
                mine = mlin_ref[h, 0, :, cols]
                top = jnp.maximum(m, mine)
                a, b = jnp.exp2(m - top), jnp.exp2(mine - top)
                inverse = 1.0 / (l * a + mlin_ref[h, 1, :, cols] * b)
                o = o * (a * inverse) + unpack(h, t) * (b * inverse)
                late_ref[:, cols] += jnp.sum(o * o, 0, keepdims=True)
            else:
                mlsend_ref[h, 0, :, cols], mlsend_ref[h, 1, :, cols] = m, l
            pack(h, t, o)

    def help_own(h):
        for t, tile in enumerate(tiles):
            queries = query_tile(t, own_query(h))
            first = noisy(h, t, queries)
            m, l, o = help_sums(h, part_of(scale, tile), first, queries, helper, blocks)
            finish_tile(h, t, o * (1.0 / l))

    def gather_hidden():
        for d in range(1, group):
            part_copy(d).wait()
        summed = part_ref[g].astype(F32)
        for d in range(1, group):
            summed = summed + part_in[d - 1].astype(F32)
        hid_ref[...] = summed.astype(BF16)

    def update_all(h):
        lax.fori_loop(0, p, lambda j, c: (own_update(j, h), c)[1], 0)

    def first_heads(h):
        @pl.when(feeds & (h + ahead < heads))
        def _():
            pass_on(h + ahead)

        @pl.when(jnp.logical_not(helps) & (h == min(1, heads - 1)))
        def _():
            gather_hidden()

        @pl.when(helps)
        def _():
            @pl.when(h >= routed)
            def _():
                lastq_copy(h).wait_recv()

            @pl.when((h >= routed) & (h < final))
            def _():
                help_last(h)
                ml_copy(h).start()
                o_copy(h).start()

            if final < heads:

                @pl.when(h >= final)
                def _():
                    help_last(h, True)
                    o_copy(h).start()

                @pl.when(h == heads - 1)
                def _():
                    for d in range(1, group):
                        late_copy(d).start()

            help_own(h)

        @pl.when(jnp.logical_not(helps))
        def _():
            own_state(h)

        @pl.when(jnp.logical_not(helps | ends))
        def _():
            update_all(h)
            finish_own(h)

    def last_routed(h):
        lax.fori_loop(0, p, lambda j, c: (arrive(j, h), c)[1], 0)
        update_all(h)
        finish_own(h)

    def decode():
        loads[7].wait()

        @pl.when(p > 0)
        def _():
            hid_copy.wait_recv()

        @pl.when(p == 0)
        def _():
            prev_ref[...] = jnp.zeros_like(prev_ref)

        now = hid_ref[...].astype(F32)
        before = prev_ref[...].astype(F32)
        width = now.shape[1]
        frame = lax.rem(lax.broadcasted_iota(jnp.int32, (rp, width), 0), FR)
        mixed = jnp.zeros((2 * rp, width), F32)
        for k in range(KT):
            late = pltpu.roll(before, k, 0) if k else before
            if k:
                cur = jnp.where(
                    frame >= k, pltpu.roll(now, k, 0), pltpu.roll(before, rp + k - FR, 0)
                )
            else:
                cur = now
            window = jnp.concatenate([cur, late], 0).astype(BF16)
            mixed = mixed + jnp.dot(window, conv_ref[k], preferred_element_type=F32)
        frames = jax.nn.silu(mixed).astype(BF16).astype(F32)
        cur, late = frames[:rp], frames[rp:]
        fade = fade_ref[0]
        aligned = jnp.zeros_like(late)
        for count in range(1, FADE + 1):
            aligned = jnp.where(fade == count, pltpu.roll(late, rp - FR + count, 0), aligned)
        active = (frame < fade) & (p > 0)
        fade_f = fade.astype(F32)
        weight = (frame.astype(F32) + 1.0) / (jnp.zeros((rp, width), F32) + fade_f + 1.0)
        mix = weight * cur + (1.0 - weight) * aligned
        dec_ref[0] = jnp.where(active, mix, cur)[:rows].astype(BF16)

    sq_ref[...] = jnp.zeros_like(sq_ref)
    late_ref[...] = jnp.zeros_like(late_ref)

    @pl.when(helps)
    def _():
        def hand_on_routed(j, carry):
            for h in range(routed):
                hand_on(j, h)
            return carry

        lax.fori_loop(0, min(blocks, 1), hand_on_routed, 0)
        gather_hidden()
        hid_copy.start()
        lax.fori_loop(min(blocks, 1), blocks, hand_on_routed, 0)

    every_head(first_heads)

    @pl.when(feeds)
    def _():
        hid_copy.start()

    @pl.when(ends)
    def _():
        def send_back(h):
            for t, tile in enumerate(tiles):
                cols = slice(tile[0], tile[0] + tile[1])
                pack(h, t, o_ref[h, :, cols])
            mlsend_ref[h, 0] = m_ref[h]
            mlsend_ref[h, 1] = l_ref[h]
            for copy in back_copies(h):
                copy.start()

        every_head(send_back, final)

    @pl.when(jnp.logical_not(helps))
    def _():
        decode()

    @pl.when(ends)
    def _():
        for h in range(routed):
            last_routed(h)
        lax.fori_loop(routed, final, lambda h, c: (finish_last(h), c)[1], 0)

    for d in range(1, group):
        stat_copy(d).start()

    @pl.when(helps)
    def _():
        decode()
        if final < heads:
            sums = late_ref[...]
            for d in range(1, group):
                late_copy(d).wait_recv()
                sums = sums + late_in[d - 1]
            late_sum[...] = sums
            sum_copy().start()

    if final < heads:

        @pl.when(ends)
        def _():
            def finish_late(h):
                o_copy(h).wait_recv()
                for t in range(len(tiles)):
                    finish_tile(h, t, unpack(h, t), False)

            every_head(finish_late, final)

    for d in range(1, group):
        stat_copy(d).wait_recv()
    squares = sq_ref[...]
    for d in range(1, group):
        squares = squares + stat_in[d - 1]

    def invert(sums):
        inv_ref[...] = lax.rsqrt(sums / (HD * heads * group) + 1e-06)

    @pl.when(jnp.logical_not(ends))
    def _():
        invert(squares)

    @pl.when(ends)
    def _():
        if final < heads:
            sum_copy().wait_recv()
            invert(squares + late_got[...])
        else:
            invert(squares)

    for d in range(1, group):
        stat_copy(d).wait_send()

    @pl.when(p < n - 1)
    def _():
        hid_copy.wait_send()

    def drain_kv(h):
        def one(j, carry):
            kv_copy(clean_hbm.at[:, 0, :, head_cols(h)], j, h).wait_send()
            return carry

        lax.fori_loop(0, p + 1, one, 0)

    @pl.when(feeds)
    def _():
        every_head(drain_kv)

    @pl.when(helps)
    def _():
        for h in range(routed):
            drain_kv(h)

        def drain(h):
            ml_copy(h).wait_send()
            o_copy(h).wait_send()

        lax.fori_loop(routed, final, lambda h, c: (drain(h), c)[1], 0)
        if final < heads:
            every_head(lambda h: o_copy(h).wait_send(), final)
            for d in range(1, group):
                late_copy(d).wait_send()
            sum_copy().wait_send()

    @pl.when(ends)
    def _():
        every_head(lambda h: lastq_copy(h).wait_send(), routed)

        def drain_back(h):
            for copy in back_copies(h):
                copy.wait_send()

        every_head(drain_back, final)


def write_out(dims, avg_ref, inv_ref, dec_ref, att_hbm, dec_hbm, att_ref, sem):
    steps, ct, heads, main = dims
    rest, split = ct - main, steps * main
    dec_copy = pltpu.make_async_copy(dec_ref, dec_hbm, sem.at[steps])
    dec_copy.start()
    turned = lambda lo, hi: jnp.transpose(jnp.broadcast_to(inv_ref[:, lo:hi], (HD, hi - lo)))
    late = turned(split, steps * ct) if rest else None
    copies = []
    for s in range(steps):
        inverse = turned(s * main, (s + 1) * main) if main else None
        spans = [(0, main, s * main)] if main else []
        if rest:
            spans.append((main, ct, split + s * rest))
        for lo, hi, at in spans:
            for h in range(heads):
                cols = slice(h * HD, (h + 1) * HD)
                att_ref[s, 0, lo:hi, cols] = (
                    avg_ref[s, 0, lo:hi, cols] * (late[at - split : at - split + hi - lo] if lo else inverse)
                ).astype(BF16)
        copy = pltpu.make_async_copy(att_ref.at[s], att_hbm.at[s], sem.at[s])
        copy.start()
        copies.append(copy)
    for copy in copies:
        copy.wait()
    dec_copy.wait()


def per_device(sizes, query, noisy_kv, clean_kv, causal_mask, step_index, finished, w_in, conv_w, fade_count):
    n, mp_n, seq_n = sizes
    group = mp_n * seq_n
    steps, _, ct, width = query.shape
    heads = width // HD
    channels = w_in.shape[1]
    rows = ct // group
    rp = -(-rows // 16) * 16
    main = ct // LANES * LANES
    total = steps * ct
    dims = (n, mp_n, seq_n, steps, ct, heads, rows, rp, main)
    vmem = pltpu.VMEM
    dma = pltpu.SemaphoreType.DMA
    hbm = pl.BlockSpec(memory_space=pltpu.HBM)
    out = pl.BlockSpec(memory_space=pltpu.VMEM)
    slots = max(n - 1, 1)
    arguments = [
        pltpu.with_memory_space_constraint(x, pltpu.HBM)
        for x in (causal_mask, step_index, query, noisy_kv, clean_kv, finished, w_in, conv_w)
    ]
    arguments.insert(2, fade_count)
    averaged, inverse, decoded = pl.pallas_call(
        functools.partial(kernel, dims),
        out_shape=(
            jax.ShapeDtypeStruct(query.shape, F32),
            jax.ShapeDtypeStruct((1, total), F32),
            jax.ShapeDtypeStruct((1, rows, channels), BF16),
        ),
        in_specs=[hbm] * 9,
        out_specs=(out, out, out),
        scratch_shapes=[
            vmem(query.shape, BF16),
            vmem(noisy_kv.shape, BF16),
            vmem(finished.shape, BF16),
            vmem(w_in.shape, BF16),
            vmem(conv_w.shape, BF16),
            vmem(clean_kv.shape, BF16),
            vmem((slots, heads, 2, ct, HD), BF16),
            vmem((heads, steps, ct, HD), BF16),
            vmem((heads, 1, total), F32),
            vmem((heads, 1, total), F32),
            vmem((heads, HD, total), F32),
            vmem((heads, total * HD // LANES, LANES), BF16),
            vmem((heads, total * HD // LANES, LANES), BF16),
            vmem((heads, 2, 1, total), F32),
            vmem((heads, 2, 1, total), F32),
            vmem((group, rp, channels), BF16),
            vmem((group - 1, rp, channels), BF16),
            vmem((rp, channels), BF16),
            vmem((rp, channels), BF16),
            vmem((1, total), F32),
            vmem((group - 1, 1, total), F32),
            vmem((1, total), F32),
            vmem((group - 1, 1, total), F32),
            vmem((1, total), F32),
            vmem((1, total), F32),
            pltpu.SMEM(causal_mask.shape, jnp.int32),
            pltpu.SMEM(step_index.shape, jnp.int32),
            pltpu.SMEM(fade_count.shape, jnp.int32),
            dma((9,)),
            dma((slots, heads)),
            dma((slots, heads)),
            dma((heads,)),
            dma((heads,)),
            dma((heads,)),
            dma((heads,)),
            dma((heads,)),
            dma((heads,)),
            dma((group - 1,)),
            dma((group - 1,)),
            dma,
            dma,
            dma((group - 1,)),
            dma((group - 1,)),
            dma((group - 1,)),
            dma((group - 1,)),
            dma((2, heads)),
            dma((2, heads)),
            dma,
            dma,
        ],
        compiler_params=pltpu.CompilerParams(
            collective_id=0, has_side_effects=True, vmem_limit_bytes=28 * 2**20
        ),
    )(*arguments)
    return pl.pallas_call(
        functools.partial(write_out, (steps, ct, heads, main)),
        out_shape=(
            jax.ShapeDtypeStruct(query.shape, BF16),
            jax.ShapeDtypeStruct(decoded.shape, BF16),
        ),
        in_specs=[out] * 3,
        out_specs=(hbm, hbm),
        scratch_shapes=[vmem(query.shape, BF16), dma((steps + 1,))],
        compiler_params=pltpu.CompilerParams(vmem_limit_bytes=8 * 2**20),
    )(averaged, inverse, decoded)


def solution(mesh):
    placed = (
        P(None, ("groups", "span"), None, ("mp", "seq")),
        P(None, None, ("groups", "span"), None, ("mp", "seq")),
        P(None, ("groups", "span"), None, ("mp", "seq")),
        P("groups", None),
        P("groups", None),
        P(("groups", "span"), None, ("mp", "seq")),
        P(("mp", "seq"), None),
        P(),
        P(("groups", "span")),
    )
    sizes = (mesh.shape["span"], mesh.shape["mp"], mesh.shape["seq"])
    return jax.shard_map(
        functools.partial(per_device, sizes),
        mesh=mesh,
        in_specs=placed,
        out_specs=(
            P(None, ("groups", "span"), None, ("mp", "seq")),
            P(("groups", "span"), ("mp", "seq"), None),
        ),
        check_vma=False,
    )
```

```python
import functools
import math

import jax
import jax.numpy as jnp
from jax import lax
from jax.experimental import pallas as pl
from jax.experimental.pallas import tpu as pltpu
from jax.sharding import PartitionSpec as P

FR = 6
HD = 128
KT = 3
FADE = 2
NSTEPS = 64
LANES = 128
MESH = pl.DeviceIdType.MESH
LOG2E = 1.4426950408889634
LOW = -1e30
F32 = jnp.float32
BF16 = jnp.bfloat16


def nt_dot(a, b):
    return lax.dot_general(a, b, (((1,), (1,)), ((), ())), preferred_element_type=F32)


def tn_dot(a, b):
    return lax.dot_general(a, b, (((0,), (0,)), ((), ())), preferred_element_type=F32)


def head_cols(h):
    return pl.ds(pl.multiple_of(h * HD, HD), HD)


def kernel(
    dims,
    mask_hbm, index_hbm, fade_hbm, query_hbm, noisy_hbm, clean_hbm, fin_hbm, win_hbm, conv_hbm,
    avg_ref, inv_ref, dec_ref,
    q_ref, noisy_ref, fin_ref, win_ref, conv_ref, own_ref, kv_ref, lastq_ref,
    m_ref, l_ref, o_ref, osend_ref, oin_ref, mlsend_ref, mlin_ref,
    part_ref, part_in, hid_ref, prev_ref, sq_ref, stat_in, late_ref, late_in, late_sum, late_got, mask_ref, index_ref, fade_ref,
    load_sem, kv_send, kv_recv, lastq_send, lastq_recv, o_send, o_recv, ml_send, ml_recv,
    part_send, part_recv, hid_send, hid_recv, stat_send, stat_recv,
    late_send, late_recv, back_send, back_recv, sum_send, sum_recv,
):
    n, mp_n, seq_n, steps, ct, heads, rows, rp, main = dims
    group = mp_n * seq_n
    rest = ct - main
    total = steps * ct
    p = lax.axis_index("span")
    g = lax.axis_index("mp") * seq_n + lax.axis_index("seq")
    last, helper = n - 1, n - 2
    feeds = p < helper
    helps = p == helper
    ends = (p == last) & (n > 1)
    blocks = max(helper, 0)
    routed = min(2, heads) if n > 1 else 0
    final = max(routed, heads - 2) if n > 1 else heads

    def peer(d):
        other = lax.rem(g + d, group)
        return other, {"mp": other // seq_n, "seq": lax.rem(other, seq_n)}

    barrier = pltpu.get_barrier_semaphore()

    @pl.when(p > 0)
    def _():
        pl.semaphore_signal(barrier, inc=1, device_id={"span": p - 1}, device_id_type=MESH)

    @pl.when(p < n - 1)
    def _():
        pl.semaphore_signal(barrier, inc=1, device_id={"span": p + 1}, device_id_type=MESH)

    for d in range(1, group):
        pl.semaphore_signal(barrier, inc=1, device_id=peer(d)[1], device_id_type=MESH)

    near = (p > 0).astype(jnp.int32) + (p < n - 1).astype(jnp.int32)
    loads = []
    for i, (src, dst) in enumerate(
        (
            (fin_hbm, fin_ref), (win_hbm, win_ref), (query_hbm, q_ref), (noisy_hbm, noisy_ref),
            (mask_hbm, mask_ref), (index_hbm, index_ref), (fade_hbm, fade_ref), (conv_hbm, conv_ref),
            (clean_hbm, own_ref),
        )
    ):
        loads.append(pltpu.make_async_copy(src, dst, load_sem.at[i]))
    for copy in loads[:2]:
        copy.start()

    pl.semaphore_wait(barrier, group - 1 + near)

    def kv_copy(src, slot, h):
        return pltpu.make_async_remote_copy(
            src_ref=src, dst_ref=kv_ref.at[slot, h], send_sem=kv_send.at[slot, h],
            recv_sem=kv_recv.at[slot, h], device_id={"span": p + 1}, device_id_type=MESH,
        )

    def own_kv_copy(h):
        return kv_copy(clean_hbm.at[:, 0, :, head_cols(h)], 0, h)

    def lastq_copy(h):
        return pltpu.make_async_remote_copy(
            src_ref=query_hbm.at[:, 0, :, head_cols(h)], dst_ref=lastq_ref.at[h],
            send_sem=lastq_send.at[h], recv_sem=lastq_recv.at[h],
            device_id={"span": p - 1}, device_id_type=MESH,
        )

    def o_copy(h):
        return pltpu.make_async_remote_copy(
            src_ref=osend_ref.at[h], dst_ref=oin_ref.at[h], send_sem=o_send.at[h],
            recv_sem=o_recv.at[h], device_id={"span": p + 1}, device_id_type=MESH,
        )

    def ml_copy(h):
        return pltpu.make_async_remote_copy(
            src_ref=mlsend_ref.at[h], dst_ref=mlin_ref.at[h], send_sem=ml_send.at[h],
            recv_sem=ml_recv.at[h], device_id={"span": p + 1}, device_id_type=MESH,
        )

    def back_copies(h):
        where = {"span": p - 1}
        return [
            pltpu.make_async_remote_copy(
                src_ref=src.at[h], dst_ref=dst.at[h], send_sem=back_send.at[i, h],
                recv_sem=back_recv.at[i, h], device_id=where, device_id_type=MESH,
            )
            for i, (src, dst) in enumerate(((mlsend_ref, mlin_ref), (osend_ref, oin_ref)))
        ]

    def late_copy(d):
        return pltpu.make_async_remote_copy(
            src_ref=late_ref, dst_ref=late_in.at[d - 1], send_sem=late_send.at[d - 1],
            recv_sem=late_recv.at[d - 1], device_id=peer(d)[1], device_id_type=MESH,
        )

    def sum_copy():
        return pltpu.make_async_remote_copy(
            src_ref=late_sum, dst_ref=late_got, send_sem=sum_send, recv_sem=sum_recv,
            device_id={"span": p + 1}, device_id_type=MESH,
        )

    def part_copy(d):
        other, where = peer(d)
        return pltpu.make_async_remote_copy(
            src_ref=part_ref.at[other], dst_ref=part_in.at[d - 1], send_sem=part_send.at[d - 1],
            recv_sem=part_recv.at[d - 1], device_id=where, device_id_type=MESH,
        )

    def stat_copy(d):
        return pltpu.make_async_remote_copy(
            src_ref=sq_ref, dst_ref=stat_in.at[d - 1], send_sem=stat_send.at[d - 1],
            recv_sem=stat_recv.at[d - 1], device_id=peer(d)[1], device_id_type=MESH,
        )

    hid_copy = pltpu.make_async_remote_copy(
        src_ref=hid_ref, dst_ref=prev_ref, send_sem=hid_send, recv_sem=hid_recv,
        device_id={"span": p + 1}, device_id_type=MESH,
    )

    def every_head(body, first=0):
        lax.fori_loop(first, heads, lambda h, c: (body(h), c)[1], 0)

    ahead = max(routed, 1)

    @pl.when(feeds)
    def _():
        for h in range(ahead):
            own_kv_copy(h).start()

    @pl.when(helps)
    def _():
        for h in range(routed):
            own_kv_copy(h).start()

    @pl.when(ends)
    def _():
        every_head(lambda h: lastq_copy(h).start(), routed)

    for copy in loads[2:8]:
        copy.start()

    @pl.when(helps)
    def _():
        loads[8].start()

    def arrive(j, h):
        kv_copy(kv_ref.at[j, h], j, h).wait_recv()

    def hand_on(j, h):
        arrive(j, h)
        kv_copy(kv_ref.at[j, h], j + 1, h).start()

    def pass_on(h):
        lax.fori_loop(0, p, lambda j, c: (hand_on(j, h), c)[1], 0)

        @pl.when((h + 1 >= ahead) & (h + 1 < heads))
        def _():
            own_kv_copy(h + 1).start()

    @pl.when(feeds)
    def _():
        for h in range(ahead):
            pass_on(h)

    loads[0].wait()
    loads[1].wait()
    partial = jnp.dot(fin_ref[0], win_ref[...], preferred_element_type=F32).astype(BF16)
    row = lax.broadcasted_iota(jnp.int32, (rp, ct), 0)
    col = lax.broadcasted_iota(jnp.int32, (rp, ct), 1)
    for o in range(group):
        pick = jnp.where((row < rows) & (col == row + o * rows), 1.0, 0.0).astype(BF16)
        part_ref[o] = jnp.dot(pick, partial, preferred_element_type=F32).astype(BF16)
    for d in range(1, group):
        part_copy(d).start()

    for i in (2, 3, 4, 5, 6):
        loads[i].wait()

    @pl.when(helps)
    def _():
        loads[8].wait()

    lane = lax.broadcasted_iota(jnp.int32, (1, total), 1)
    split = steps * main
    step_of = jnp.zeros((1, total), jnp.int32)
    for s in range(1, steps):
        step_of = step_of + (
            ((lane >= s * main) & (lane < split)) | (lane >= split + s * rest)
        ).astype(jnp.int32)

    def scale_row(segment):
        indices = jnp.zeros((1, total), F32)
        for s in range(steps):
            indices = jnp.where(step_of == s, index_ref[segment, s].astype(F32), indices)
        fraction = 1.0 - indices / NSTEPS
        level = 3.0 * fraction / (1.0 + 2.0 * fraction)
        return (0.5 + level) * (LOG2E / math.sqrt(HD))

    scale = scale_row(p)
    last_scale = scale_row(last)

    whole = [(s, 0, main) for s in range(steps if main else 0)]
    tail = [(s, main, ct) for s in range(steps if rest else 0)]
    tiles = [(0, total, whole + tail)]

    def query_tile(t, row):
        return jnp.concatenate([row(*piece) for piece in tiles[t][2]], 0)

    def own_query(h):
        return lambda s, lo, hi: q_ref[s, 0, lo:hi, head_cols(h)]

    def last_query(h):
        return lambda s, lo, hi: lastq_ref[h, s, lo:hi, :]

    def part_of(ref, tile):
        return ref[:, tile[0] : tile[0] + tile[1]]

    def one_pass(c, scored, old=None):
        tops = []
        for scores, _, visible in scored:
            top = scores.max(0, keepdims=True) * c
            tops.append(top if visible is None else jnp.where(visible > 0, top, LOW))
        m = functools.reduce(jnp.maximum, tops)
        if old is not None:
            m = jnp.maximum(m, old[0])
        l, o, weights, values = 0.0, 0.0, [], []
        for scores, held, visible in scored:
            base = m if visible is None else jnp.where(visible > 0, m, -LOW)
            w = jnp.exp2(scores * c - base)
            l = l + w.sum(0, keepdims=True)
            if callable(held):
                o = o + held(w)
            else:
                weights.append(w.astype(BF16))
                values.append(held)
        if values:
            o = o + tn_dot(jnp.concatenate(values, 0), jnp.concatenate(weights, 0))
        if old is not None:
            factor = jnp.exp2(old[0] - m)
            l = l + old[1] * factor
            o = o + old[2] * factor
        return m, l, o

    def plain(keys, values, queries, visible):
        return nt_dot(keys, queries), values, visible

    def noisy(h, t, queries):
        keys = lambda s: noisy_ref[s, 0, 0, :, head_cols(h)]
        values = lambda s: noisy_ref[s, 1, 0, :, head_cols(h)]
        cut = lambda k: slice(k * main, (k + 1) * main)
        scores = [nt_dot(keys(k), queries[cut(k)]) for k, _, _ in whole]
        if tail:
            owner = lax.broadcasted_iota(jnp.int32, (ct, steps * rest), 1) // rest
            every = nt_dot(jnp.concatenate([keys(s) for s in range(steps)], 0), queries[split:])
            picked = every[0:ct]
            for s in range(1, steps):
                picked = jnp.where(owner == s, every[s * ct : (s + 1) * ct], picked)
            scores.append(picked)

        def weigh(w):
            o = [tn_dot(values(k), w[:, cut(k)].astype(BF16)) for k, _, _ in whole]
            if tail:
                late = w[:, split:]
                mine = [jnp.where(owner == s, late, 0.0).astype(BF16) for s in range(steps)]
                o.append(
                    tn_dot(jnp.concatenate([values(s) for s in range(steps)], 0), jnp.concatenate(mine, 0))
                )
            return jnp.concatenate(o, 1)

        return jnp.concatenate(scores, 1), weigh, None

    def own_state(h):
        for t, tile in enumerate(tiles):
            queries = query_tile(t, own_query(h))
            m, l, o = one_pass(part_of(scale, tile), [noisy(h, t, queries)])
            cols = slice(tile[0], tile[0] + tile[1])
            m_ref[h, :, cols], l_ref[h, :, cols], o_ref[h, :, cols] = m, l, o

    def own_update(j, h):
        visible = mask_ref[p, p - 1 - j]
        for t, tile in enumerate(tiles):
            queries = query_tile(t, own_query(h))
            cols = slice(tile[0], tile[0] + tile[1])
            old = m_ref[h, :, cols], l_ref[h, :, cols], o_ref[h, :, cols]
            block = plain(kv_ref[j, h, 0], kv_ref[j, h, 1], queries, visible)
            m, l, o = one_pass(part_of(scale, tile), [block], old)
            m_ref[h, :, cols], l_ref[h, :, cols], o_ref[h, :, cols] = m, l, o

    def finish_tile(h, t, averaged, count=True):
        lo, width, pieces = tiles[t]
        if count:
            sq_ref[:, lo : lo + width] += jnp.sum(averaged * averaged, 0, keepdims=True)
        turned = jnp.transpose(averaged)
        at = 0
        for s, first, end in pieces:
            avg_ref[s, 0, first:end, head_cols(h)] = turned[at : at + end - first]
            at += end - first

    def finish_own(h):
        for t, tile in enumerate(tiles):
            cols = slice(tile[0], tile[0] + tile[1])
            finish_tile(h, t, o_ref[h, :, cols] * (1.0 / l_ref[h, :, cols]))

    fold = LANES // (steps * rest) if rest else 1

    def pack(h, t, o):
        for i in range(split // LANES):
            osend_ref[h, i * HD : (i + 1) * HD, :] = o[:, i * LANES : (i + 1) * LANES].astype(BF16)
        if rest:
            high, at = HD // fold, split // LANES * HD
            pieces = [o[i * high : (i + 1) * high, split:] for i in range(fold)]
            osend_ref[h, at : at + high, :] = jnp.concatenate(pieces, 1).astype(BF16)

    def unpack(h, t):
        pieces = [
            oin_ref[h, i * HD : (i + 1) * HD, :].astype(F32) for i in range(split // LANES)
        ]
        if rest:
            high, at, width = HD // fold, split // LANES * HD, steps * rest
            held = oin_ref[h, at : at + high, :].astype(F32)
            pieces.append(
                jnp.concatenate([held[:, i * width : (i + 1) * width] for i in range(fold)], 0)
            )
        return jnp.concatenate(pieces, 1)

    def finish_last(h):
        ml_copy(h).wait_recv()
        o_copy(h).wait_recv()
        for t, tile in enumerate(tiles):
            cols = slice(tile[0], tile[0] + tile[1])
            mine, theirs = m_ref[h, :, cols], mlin_ref[h, 0, :, cols]
            m = jnp.maximum(mine, theirs)
            a, b = jnp.exp2(mine - m), jnp.exp2(theirs - m)
            inverse = 1.0 / (l_ref[h, :, cols] * a + mlin_ref[h, 1, :, cols] * b)
            finish_tile(h, t, o_ref[h, :, cols] * (a * inverse) + unpack(h, t) * (b * inverse))

    def arrived(h, j, queries, segment):
        visible = mask_ref[segment, helper - 1 - j]
        return plain(kv_ref[j, h, 0], kv_ref[j, h, 1], queries, visible)

    def help_sums(h, c, first, queries, segment, count):
        together = min(count, 3)
        held = [first] + [arrived(h, j, queries, segment) for j in range(together)]
        sums = one_pass(c, held)
        if count > together:
            sums = lax.fori_loop(
                together, count,
                lambda j, so_far: one_pass(c, [arrived(h, j, queries, segment)], so_far), sums,
            )
        return sums

    def help_last(h, closing=False):
        early = max(blocks - 1, 0)
        lax.fori_loop(0, early, lambda j, c: (arrive(j, h), c)[1], 0)
        for t, tile in enumerate(tiles):
            queries = query_tile(t, last_query(h))
            cols = slice(tile[0], tile[0] + tile[1])
            own = plain(
                own_ref[0, 0, :, head_cols(h)], own_ref[1, 0, :, head_cols(h)], queries,
                mask_ref[last, helper],
            )
            m, l, o = help_sums(h, part_of(last_scale, tile), own, queries, last, early)
            m_ref[h, :, cols], l_ref[h, :, cols], o_ref[h, :, cols] = m, l, o
        if blocks:
            arrive(blocks - 1, h)
        if closing:
            for copy in back_copies(h):
                copy.wait_recv()
        for t, tile in enumerate(tiles):
            queries = query_tile(t, last_query(h))
            cols = slice(tile[0], tile[0] + tile[1])
            m, l, o = m_ref[h, :, cols], l_ref[h, :, cols], o_ref[h, :, cols]
            if blocks:
                block = arrived(h, blocks - 1, queries, last)
                m, l, o = one_pass(part_of(last_scale, tile), [block], (m, l, o))
            if closing:
                mine = mlin_ref[h, 0, :, cols]
                top = jnp.maximum(m, mine)
                a, b = jnp.exp2(m - top), jnp.exp2(mine - top)
                inverse = 1.0 / (l * a + mlin_ref[h, 1, :, cols] * b)
                o = o * (a * inverse) + unpack(h, t) * (b * inverse)
                late_ref[:, cols] += jnp.sum(o * o, 0, keepdims=True)
            else:
                mlsend_ref[h, 0, :, cols], mlsend_ref[h, 1, :, cols] = m, l
            pack(h, t, o)

    def help_own(h):
        for t, tile in enumerate(tiles):
            queries = query_tile(t, own_query(h))
            first = noisy(h, t, queries)
            m, l, o = help_sums(h, part_of(scale, tile), first, queries, helper, blocks)
            finish_tile(h, t, o * (1.0 / l))

    def gather_hidden():
        for d in range(1, group):
            part_copy(d).wait()
        summed = part_ref[g].astype(F32)
        for d in range(1, group):
            summed = summed + part_in[d - 1].astype(F32)
        hid_ref[...] = summed.astype(BF16)

    def update_all(h):
        lax.fori_loop(0, p, lambda j, c: (own_update(j, h), c)[1], 0)

    def first_heads(h):
        @pl.when(feeds & (h + ahead < heads))
        def _():
            pass_on(h + ahead)

        @pl.when(jnp.logical_not(helps) & (h == min(1, heads - 1)))
        def _():
            gather_hidden()

        @pl.when(helps)
        def _():
            @pl.when(h >= routed)
            def _():
                lastq_copy(h).wait_recv()

            @pl.when((h >= routed) & (h < final))
            def _():
                help_last(h)
                ml_copy(h).start()
                o_copy(h).start()

            if final < heads:

                @pl.when(h >= final)
                def _():
                    help_last(h, True)
                    o_copy(h).start()

                @pl.when(h == heads - 1)
                def _():
                    for d in range(1, group):
                        late_copy(d).start()

            help_own(h)

        @pl.when(jnp.logical_not(helps))
        def _():
            own_state(h)

        @pl.when(jnp.logical_not(helps | ends))
        def _():
            update_all(h)
            finish_own(h)

    def last_routed(h):
        lax.fori_loop(0, p, lambda j, c: (arrive(j, h), c)[1], 0)
        update_all(h)
        finish_own(h)

    def decode():
        loads[7].wait()

        @pl.when(p > 0)
        def _():
            hid_copy.wait_recv()

        @pl.when(p == 0)
        def _():
            prev_ref[...] = jnp.zeros_like(prev_ref)

        now = hid_ref[...].astype(F32)
        before = prev_ref[...].astype(F32)
        width = now.shape[1]
        frame = lax.rem(lax.broadcasted_iota(jnp.int32, (rp, width), 0), FR)
        mixed = jnp.zeros((2 * rp, width), F32)
        for k in range(KT):
            late = pltpu.roll(before, k, 0) if k else before
            if k:
                cur = jnp.where(
                    frame >= k, pltpu.roll(now, k, 0), pltpu.roll(before, rp + k - FR, 0)
                )
            else:
                cur = now
            window = jnp.concatenate([cur, late], 0).astype(BF16)
            mixed = mixed + jnp.dot(window, conv_ref[k], preferred_element_type=F32)
        frames = jax.nn.silu(mixed).astype(BF16).astype(F32)
        cur, late = frames[:rp], frames[rp:]
        fade = fade_ref[0]
        aligned = jnp.zeros_like(late)
        for count in range(1, FADE + 1):
            aligned = jnp.where(fade == count, pltpu.roll(late, rp - FR + count, 0), aligned)
        active = (frame < fade) & (p > 0)
        fade_f = fade.astype(F32)
        weight = (frame.astype(F32) + 1.0) / (jnp.zeros((rp, width), F32) + fade_f + 1.0)
        mix = weight * cur + (1.0 - weight) * aligned
        dec_ref[0] = jnp.where(active, mix, cur)[:rows].astype(BF16)

    sq_ref[...] = jnp.zeros_like(sq_ref)
    late_ref[...] = jnp.zeros_like(late_ref)

    @pl.when(helps)
    def _():
        def hand_on_routed(j, carry):
            for h in range(routed):
                hand_on(j, h)
            return carry

        lax.fori_loop(0, min(blocks, 1), hand_on_routed, 0)
        gather_hidden()
        hid_copy.start()
        lax.fori_loop(min(blocks, 1), blocks, hand_on_routed, 0)

    every_head(first_heads)

    @pl.when(feeds)
    def _():
        hid_copy.start()

    @pl.when(ends)
    def _():
        def send_back(h):
            for t, tile in enumerate(tiles):
                cols = slice(tile[0], tile[0] + tile[1])
                pack(h, t, o_ref[h, :, cols])
            mlsend_ref[h, 0] = m_ref[h]
            mlsend_ref[h, 1] = l_ref[h]
            for copy in back_copies(h):
                copy.start()

        every_head(send_back, final)

    @pl.when(jnp.logical_not(helps))
    def _():
        decode()

    @pl.when(ends)
    def _():
        for h in range(routed):
            last_routed(h)
        lax.fori_loop(routed, final, lambda h, c: (finish_last(h), c)[1], 0)

    for d in range(1, group):
        stat_copy(d).start()

    @pl.when(helps)
    def _():
        decode()
        if final < heads:
            sums = late_ref[...]
            for d in range(1, group):
                late_copy(d).wait_recv()
                sums = sums + late_in[d - 1]
            late_sum[...] = sums
            sum_copy().start()

    @pl.when(ends)
    def _():
        every_head(lambda h: lastq_copy(h).wait_send(), routed)

        def drain_back(h):
            for copy in back_copies(h):
                copy.wait_send()

        every_head(drain_back, final)

    if final < heads:

        @pl.when(ends)
        def _():
            def finish_late(h):
                o_copy(h).wait_recv()
                for t in range(len(tiles)):
                    finish_tile(h, t, unpack(h, t), False)

            every_head(finish_late, final)

    for d in range(1, group):
        stat_copy(d).wait_recv()
    squares = sq_ref[...]
    for d in range(1, group):
        squares = squares + stat_in[d - 1]

    def invert(sums):
        inv_ref[...] = lax.rsqrt(sums / (HD * heads * group) + 1e-06)

    @pl.when(jnp.logical_not(ends))
    def _():
        invert(squares)

    @pl.when(ends)
    def _():
        if final < heads:
            sum_copy().wait_recv()
            invert(squares + late_got[...])
        else:
            invert(squares)

    for d in range(1, group):
        stat_copy(d).wait_send()

    @pl.when(p < n - 1)
    def _():
        hid_copy.wait_send()

    def drain_kv(h):
        def one(j, carry):
            kv_copy(clean_hbm.at[:, 0, :, head_cols(h)], j, h).wait_send()
            return carry

        lax.fori_loop(0, p + 1, one, 0)

    @pl.when(feeds)
    def _():
        every_head(drain_kv)

    @pl.when(helps)
    def _():
        for h in range(routed):
            drain_kv(h)

        def drain(h):
            ml_copy(h).wait_send()
            o_copy(h).wait_send()

        lax.fori_loop(routed, final, lambda h, c: (drain(h), c)[1], 0)
        if final < heads:
            every_head(lambda h: o_copy(h).wait_send(), final)
            for d in range(1, group):
                late_copy(d).wait_send()
            sum_copy().wait_send()


def write_out(dims, avg_ref, inv_ref, dec_ref, att_hbm, dec_hbm, att_ref, sem):
    steps, ct, heads, main = dims
    rest, split = ct - main, steps * main
    dec_copy = pltpu.make_async_copy(dec_ref, dec_hbm, sem.at[steps])
    dec_copy.start()
    turned = lambda lo, hi: jnp.transpose(jnp.broadcast_to(inv_ref[:, lo:hi], (HD, hi - lo)))
    late = turned(split, steps * ct) if rest else None
    copies = []
    for s in range(steps):
        inverse = turned(s * main, (s + 1) * main) if main else None
        spans = [(0, main, s * main)] if main else []
        if rest:
            spans.append((main, ct, split + s * rest))
        for lo, hi, at in spans:
            for h in range(heads):
                cols = slice(h * HD, (h + 1) * HD)
                att_ref[s, 0, lo:hi, cols] = (
                    avg_ref[s, 0, lo:hi, cols] * (late[at - split : at - split + hi - lo] if lo else inverse)
                ).astype(BF16)
        copy = pltpu.make_async_copy(att_ref.at[s], att_hbm.at[s], sem.at[s])
        copy.start()
        copies.append(copy)
    for copy in copies:
        copy.wait()
    dec_copy.wait()


def per_device(sizes, query, noisy_kv, clean_kv, causal_mask, step_index, finished, w_in, conv_w, fade_count):
    n, mp_n, seq_n = sizes
    group = mp_n * seq_n
    steps, _, ct, width = query.shape
    heads = width // HD
    channels = w_in.shape[1]
    rows = ct // group
    rp = -(-rows // 16) * 16
    main = ct // LANES * LANES
    total = steps * ct
    dims = (n, mp_n, seq_n, steps, ct, heads, rows, rp, main)
    vmem = pltpu.VMEM
    dma = pltpu.SemaphoreType.DMA
    hbm = pl.BlockSpec(memory_space=pltpu.HBM)
    out = pl.BlockSpec(memory_space=pltpu.VMEM)
    slots = max(n - 1, 1)
    arguments = [
        pltpu.with_memory_space_constraint(x, pltpu.HBM)
        for x in (causal_mask, step_index, query, noisy_kv, clean_kv, finished, w_in, conv_w)
    ]
    arguments.insert(2, fade_count)
    averaged, inverse, decoded = pl.pallas_call(
        functools.partial(kernel, dims),
        out_shape=(
            jax.ShapeDtypeStruct(query.shape, F32),
            jax.ShapeDtypeStruct((1, total), F32),
            jax.ShapeDtypeStruct((1, rows, channels), BF16),
        ),
        in_specs=[hbm] * 9,
        out_specs=(out, out, out),
        scratch_shapes=[
            vmem(query.shape, BF16),
            vmem(noisy_kv.shape, BF16),
            vmem(finished.shape, BF16),
            vmem(w_in.shape, BF16),
            vmem(conv_w.shape, BF16),
            vmem(clean_kv.shape, BF16),
            vmem((slots, heads, 2, ct, HD), BF16),
            vmem((heads, steps, ct, HD), BF16),
            vmem((heads, 1, total), F32),
            vmem((heads, 1, total), F32),
            vmem((heads, HD, total), F32),
            vmem((heads, total * HD // LANES, LANES), BF16),
            vmem((heads, total * HD // LANES, LANES), BF16),
            vmem((heads, 2, 1, total), F32),
            vmem((heads, 2, 1, total), F32),
            vmem((group, rp, channels), BF16),
            vmem((group - 1, rp, channels), BF16),
            vmem((rp, channels), BF16),
            vmem((rp, channels), BF16),
            vmem((1, total), F32),
            vmem((group - 1, 1, total), F32),
            vmem((1, total), F32),
            vmem((group - 1, 1, total), F32),
            vmem((1, total), F32),
            vmem((1, total), F32),
            pltpu.SMEM(causal_mask.shape, jnp.int32),
            pltpu.SMEM(step_index.shape, jnp.int32),
            pltpu.SMEM(fade_count.shape, jnp.int32),
            dma((9,)),
            dma((slots, heads)),
            dma((slots, heads)),
            dma((heads,)),
            dma((heads,)),
            dma((heads,)),
            dma((heads,)),
            dma((heads,)),
            dma((heads,)),
            dma((group - 1,)),
            dma((group - 1,)),
            dma,
            dma,
            dma((group - 1,)),
            dma((group - 1,)),
            dma((group - 1,)),
            dma((group - 1,)),
            dma((2, heads)),
            dma((2, heads)),
            dma,
            dma,
        ],
        compiler_params=pltpu.CompilerParams(
            collective_id=0, has_side_effects=True, vmem_limit_bytes=28 * 2**20
        ),
    )(*arguments)
    return pl.pallas_call(
        functools.partial(write_out, (steps, ct, heads, main)),
        out_shape=(
            jax.ShapeDtypeStruct(query.shape, BF16),
            jax.ShapeDtypeStruct(decoded.shape, BF16),
        ),
        in_specs=[out] * 3,
        out_specs=(hbm, hbm),
        scratch_shapes=[vmem(query.shape, BF16), dma((steps + 1,))],
        compiler_params=pltpu.CompilerParams(vmem_limit_bytes=8 * 2**20),
    )(averaged, inverse, decoded)


def solution(mesh):
    placed = (
        P(None, ("groups", "span"), None, ("mp", "seq")),
        P(None, None, ("groups", "span"), None, ("mp", "seq")),
        P(None, ("groups", "span"), None, ("mp", "seq")),
        P("groups", None),
        P("groups", None),
        P(("groups", "span"), None, ("mp", "seq")),
        P(("mp", "seq"), None),
        P(),
        P(("groups", "span")),
    )
    sizes = (mesh.shape["span"], mesh.shape["mp"], mesh.shape["seq"])
    return jax.shard_map(
        functools.partial(per_device, sizes),
        mesh=mesh,
        in_specs=placed,
        out_specs=(
            P(None, ("groups", "span"), None, ("mp", "seq")),
            P(("groups", "span"), ("mp", "seq"), None),
        ),
        check_vma=False,
    )
```
